512 devices in a mesh: nest: 8 (over x, z_hi), gx: 8 (over y), gy: 8 (over z_lo, core).
Axes of the slice: x: 4, y: 8, z: 8 (z_hi: 2, z_lo: 4; z = z_hi * 4 + z_lo), core: 2. Of those that a mesh axis runs over, the one named last changes fastest.
Arguments:
- state: float32 [8, 4, 8, 128, 1024], P('nest', None, None, 'gx', 'gy'), may hold values from -6 to 6
- metric: float32 [8, 3, 128, 1024], P('nest', None, 'gx', 'gy'), may hold values from -1.2 to 1.4, as said below
- placement: int32 [7, 2], replicated, may hold values from 0 to 682, as said below
- zones: int32 [7, 4], replicated, may hold values from 2 to 5
Outputs:
- new_state: float32 [8, 4, 8, 128, 1024], P('nest', None, None, 'gx', 'gy')
The draws below stay inside these ranges and needn't reach their ends.
Inputs may be any that keep to these rules, and one draw needn't show every extreme that they name: metric[:, 0] and metric[:, 1] are terrain slopes; metric[:, 2] is the column stretch, between 0.6 and 1.4. placement[n] = (ox, oy) with ox <= 85 and oy <= 682.
All inputs are finite; a program needn't handle non-finite values.
Results may differ from the reference program's by a relative error of at most 0.0003.
Values sent between devices are 32-bit elements; how exact they have to be, the bound alone decides.
No kernel may reach another device: no remote copies, remote signals or barrier semaphores. Data moves between devices by JAX's collectives and lax.ppermute only.
A program may use at most 64 MiB of HBM per device.

```python
import jax
import jax.numpy as jnp
from jax import lax

L = 8
SUB = 4
R = 3
W_MAX = 5
NESTS = 7
NX = 128
NY = 1024
FX = 43
FY = 342
N_NEST = 8


def draw_metric(key, part):
    key_slope, key_stretch = jax.random.split(key)
    count = NESTS + 1
    slopes = 0.4 * jax.random.truncated_normal(key_slope, -3.0, 3.0, (count, 2, NX, NY), jnp.float32)
    stretch = jax.random.uniform(key_stretch, (count, 1, NX, NY), jnp.float32, 0.6, 1.4)
    return jnp.concatenate([slopes, stretch], 1)


def draw_placement(key, part):
    key_x, key_y, key_far = jax.random.split(key, 3)
    place_x = jax.random.randint(key_x, (NESTS,), 0, NX - FX + 1)
    place_y = jax.random.randint(key_y, (NESTS,), 0, NY - FY + 1)
    far_nest = jax.random.randint(key_far, (), 0, NESTS)
    which = jnp.arange(NESTS) == far_nest
    place_x = jnp.where(which, NX - FX, place_x)
    place_y = jnp.where(which, NY - FY, place_y)
    return jnp.stack([place_x, place_y], 1).astype(jnp.int32)


def draw_zones(key, part):
    key_width, key_pick = jax.random.split(key)
    widths = jax.random.randint(key_width, (NESTS, 4), 2, W_MAX + 1)
    chosen = jax.random.randint(key_pick, (), 0, NESTS * 4)
    slot_index = jnp.arange(NESTS * 4).reshape(NESTS, 4)
    return jnp.where(slot_index == chosen, W_MAX, widths).astype(jnp.int32)


def block_scale(stream_key, extent, shards, low, high):
    def one(position, parts):
        heights = jax.random.uniform(jax.random.fold_in(jax.random.fold_in(stream_key, 6), position), (parts,), jnp.float32, low / len(shards), high / len(shards))
        return jnp.repeat(jnp.exp(heights), extent[position] // parts).reshape((-1,) + (1,) * (len(extent) - position - 1))

    gain = one(*shards[0])
    for cut in shards[1:]:
        gain = gain * one(*cut)
    return gain


def bell_draw(rng, shape, deviation, most, cuts=(), kind=jnp.bfloat16):
    factor_of = block_scale(rng, shape, cuts, -0.22, 0.18) if cuts else 1.0
    result = jax.random.normal(rng, shape, jnp.float32) * deviation * factor_of
    return jnp.minimum(jnp.maximum(result, -most), most).astype(kind)


def setup_inputs(seed: int = 0) -> dict:
    seeds = jax.random.split(jax.random.key(seed), 5)
    state = bell_draw(seeds[0], (N_NEST, 4, L, NX, NY), 1.0, 6.0, ((0, 8), (3, 8), (4, 8)), jnp.float32)
    metric = draw_metric(jax.random.fold_in(seeds[4], 71), 0)
    placement = draw_placement(jax.random.fold_in(seeds[4], 71), 0)
    zones = draw_zones(jax.random.fold_in(seeds[4], 71), 0)
    return {"state": state, "metric": metric, "placement": placement, "zones": zones}


def centred_x(field):
    padded = jnp.pad(field, ((0, 0), (1, 1), (0, 0)))
    return (padded[:, 2:] - padded[:, :-2]) * 0.5


def centred_y(field):
    padded = jnp.pad(field, ((0, 0), (0, 0), (1, 1)))
    return (padded[:, :, 2:] - padded[:, :, :-2]) * 0.5


def vertical(field):
    upper = jnp.concatenate([field[1:], field[-1:]], 0)
    lower = jnp.concatenate([field[:1], field[:-1]], 0)
    return (upper - lower) * 0.5


def edge_weight(zone_width, row_index, col_index, total_x, total_y):
    widths = zone_width.astype(jnp.float32)
    row_pos = row_index.astype(jnp.float32)[:, None]
    col_pos = col_index.astype(jnp.float32)[None, :]
    dists = (row_pos, (total_x - 1) - row_pos, col_pos, (total_y - 1) - col_pos)
    weight = jnp.zeros((row_index.shape[0], col_index.shape[0]), jnp.float32)
    for edge in range(4):
        weight = jnp.maximum(weight, jnp.maximum((widths[edge] - dists[edge]) / widths[edge], 0.0))
    return weight


def advance(pair):
    fields, terrain = pair
    sigma_col = (1.0 - (jnp.arange(L, dtype=jnp.float32) + 0.5) / L)[:, None, None]
    wind_x, wind_y, updraft, pressure = fields[0], fields[1], fields[2], fields[3]
    slope_x, slope_y, stretch = terrain[0], terrain[1], terrain[2]
    for substep in range(SUB):
        press_z = vertical(pressure) / stretch
        wind_x = wind_x - 0.5 * (centred_x(pressure) - sigma_col * slope_x * press_z)
        wind_y = wind_y - 0.5 * (centred_y(pressure) - sigma_col * slope_y * press_z)
        updraft = updraft - 0.5 * press_z
        spread = centred_x(wind_x) + centred_y(wind_y)
        spread = spread - sigma_col * (slope_x * vertical(wind_x) + slope_y * vertical(wind_y)) / stretch + vertical(updraft) / stretch
        pressure = pressure - 0.5 * spread
    return jnp.stack([wind_x, wind_y, updraft, pressure])


def reference(state, metric, placement, zones):
    advanced = lax.map(advance, (state, metric))
    parent = state[NESTS]
    parent_three = jnp.stack([parent[0], parent[1], parent[3]])
    row_index = jnp.arange(NX, dtype=jnp.int32)
    col_index = jnp.arange(NY, dtype=jnp.int32)

    def blend(items):
        fields, place, zone_width = items
        src_rows = (place[0] + row_index // R).astype(jnp.int32)
        src_cols = (place[1] + col_index // R).astype(jnp.int32)
        target = jnp.take(jnp.take(parent_three, src_rows, axis=2), src_cols, axis=3)
        weight = edge_weight(zone_width, row_index, col_index, NX, NY)
        moved = jnp.stack([fields[0], fields[1], fields[3]])
        blended = moved + weight * (target - moved)
        return jnp.stack([blended[0], blended[1], fields[2], blended[2]])

    nested = lax.map(blend, (advanced[:NESTS], placement, zones))
    return jnp.concatenate([nested, advanced[NESTS:]], 0)
```

```python
import jax
import jax.numpy as jnp
from jax import lax
from jax.experimental import pallas as pl
from jax.experimental.pallas import tpu as pltpu
from jax.sharding import PartitionSpec as P

SUB = 4
R = 3
W_MAX = 5
L = 8
NESTS = 7
HALO = 8
ROWS = 16
LANES = 128
PLANES = 4 * L + 3
SLOT = 64
X_ROWS = 48
N_X = 128
N_Y = 1024
EAST = (N_X - 1) // R - 1
NORTH = (N_Y - 1) // R - 2
F32 = jnp.float32
HIGH = lax.Precision.HIGHEST

VMEM_SPEC = pl.BlockSpec(memory_space=pltpu.VMEM)
SMEM_SPEC = pl.BlockSpec(memory_space=pltpu.SMEM)


def iota(shape, dim):
    return lax.broadcasted_iota(jnp.int32, shape, dim)


def plane_row(state, metric, plane, row, count):
    if plane < 4 * L:
        return state[plane * ROWS + row : plane * ROWS + row + count, :]
    start = (plane - 4 * L) * ROWS + row
    return metric[start : start + count, :]


def pack_kernel(state, metric, placement, slots, left, right):
    gx = lax.axis_index("gx")
    gy = lax.axis_index("gy")
    rows_n = iota((24, LANES), 0)
    first = jnp.zeros((24, LANES), jnp.int32)
    for n in range(NESTS):
        low = placement[n, 0] - ROWS * gx
        base = jnp.where((low >= -1) & (low < ROWS), low, low + EAST)
        for a in range(2):
            row = jnp.clip(base + a, 0, ROWS - 1)
            out = n * SLOT + a * 24
            slots[out : out + 16, :] = state[pl.ds(row, 16, stride=ROWS), :]
            slots[out + 16 : out + 24, :] = state[pl.ds(24 * ROWS + row, 8, stride=ROWS), :]
        low = placement[n, 1] - LANES * gy
        base = jnp.where((low >= -1) & (low < LANES), low, low + NORTH)
        first = jnp.where((rows_n >= 3 * n) & (rows_n < 3 * n + 3), base + rows_n - 3 * n, first)
    pick = (iota((24, LANES), 1) == first).astype(F32)
    for t in range(3):
        start = (0, 128, 384)[t]
        cols = lax.dot_general(
            pick, state[start : start + 128, :], (((1,), (1,)), ((), ())), precision=HIGH, preferred_element_type=F32
        )
        for n in range(NESTS):
            slots[n * SLOT + X_ROWS + 3 * t : n * SLOT + X_ROWS + 3 * t + 3, :] = cols[3 * n : 3 * n + 3, :]
    lane = iota((8, LANES), 1) // 8
    for rt in range(2):
        for group in range(3):
            left_sum = jnp.zeros((8, LANES), F32)
            right_sum = jnp.zeros((8, LANES), F32)
            for s in range(16):
                plane = group * 16 + s
                if plane >= PLANES:
                    break
                value = plane_row(state, metric, plane, rt * 8, 8)
                left_sum = jnp.where(lane == s, pltpu.roll(value, 8 * s, 1) if s else value, left_sum)
                shift = (8 * s + 8) % LANES
                right_sum = jnp.where(lane == s, pltpu.roll(value, shift, 1) if shift else value, right_sum)
            at = (rt * 3 + group) * 8
            left[at : at + 8, :] = left_sum
            right[at : at + 8, :] = right_sum


def join_kernel(state, metric, from_left, from_right, up, down):
    for plane in range(PLANES):
        up[plane * 8 : plane * 8 + 8, :] = plane_row(state, metric, plane, 0, 8)
        down[plane * 8 : plane * 8 + 8, :] = plane_row(state, metric, plane, 8, 8)
    at = PLANES * 8
    up[at : at + 24, :] = from_left[0:24, :]
    up[at + 24 : at + 48, :] = from_right[0:24, :]
    down[at : at + 24, :] = from_left[24:48, :]
    down[at + 24 : at + 48, :] = from_right[24:48, :]


def next_col(centre, halo, lane):
    edge = lane == 0
    return (
        pltpu.roll(jnp.where(edge, halo, centre), LANES - 1, 1),
        pltpu.roll(jnp.where(edge, centre, halo), LANES - 1, 1),
    )


def prev_col(centre, halo, lane):
    edge = lane == LANES - 1
    return pltpu.roll(jnp.where(edge, halo, centre), 1, 1), pltpu.roll(jnp.where(edge, centre, halo), 1, 1)


EXT = ROWS + 2 * HALO


def advance_kernel(state, metric, from_left, from_right, from_up, from_down, out, wide, terrain):
    gx = lax.axis_index("gx")
    gy = lax.axis_index("gy")
    lane8 = iota((8, LANES), 1)
    at = PLANES * 8

    def unpack(ref_left, left_at, ref_right, right_at, plane):
        group, s = divmod(plane, 16)
        right_part = pltpu.roll(ref_right[right_at + 8 * group : right_at + 8 * group + 8, :], (LANES - 8 * s) % LANES, 1)
        left_part = pltpu.roll(ref_left[left_at + 8 * group : left_at + 8 * group + 8, :], (120 - 8 * s) % LANES, 1)
        return jnp.where(lane8 < 8, right_part, jnp.where(lane8 >= 120, left_part, 0.0))

    def store(plane, row, centre, halo):
        if plane < 4 * L:
            wide[plane, 0, row : row + 8, :] = centre
            wide[plane, 1, row : row + 8, :] = halo
        else:
            terrain[plane - 4 * L, 0, row : row + 8, :] = centre
            terrain[plane - 4 * L, 1, row : row + 8, :] = halo

    for plane in range(PLANES):
        store(plane, 0, from_up[plane * 8 : plane * 8 + 8, :], unpack(from_up, at, from_up, at + 24, plane))
        for rt in range(2):
            store(
                plane,
                8 + 8 * rt,
                plane_row(state, metric, plane, rt * 8, 8),
                unpack(from_left, 24 * rt, from_right, 24 * rt, plane),
            )
        store(plane, 24, from_down[plane * 8 : plane * 8 + 8, :], unpack(from_down, at, from_down, at + 24, plane))

    row = iota((EXT, LANES), 0) + ROWS * gx - HALO
    lane = iota((EXT, LANES), 1)
    row_in = (row >= 0) & (row < N_X)
    last = lax.axis_size("gy") - 1
    halo_in = row_in & (((lane < 8) & (gy < last)) | ((lane >= 120) & (gy > 0)))
    for tile, inside in ((0, row_in), (1, halo_in)):
        inverse = 1.0 / jnp.where(inside, terrain[2, tile], 1.0)
        terrain[2, tile] = inverse
        terrain[3, tile] = jnp.where(inside, 0.5, 0.0)

    def substep(_, carry):
        for k in range(L):
            up, low = min(k + 1, L - 1), max(k - 1, 0)
            sigma = 1.0 - (k + 0.5) / L
            centre, halo = wide[24 + k, 0], wide[24 + k, 1]
            east = next_col(centre, halo, lane)
            west = prev_col(centre, halo, lane)
            for tile in range(2):
                here = (centre, halo)[tile]
                step = terrain[3, tile]
                press_z = (wide[24 + up, tile] - wide[24 + low, tile]) * (0.5 * terrain[2, tile])
                grad_x = (pltpu.roll(here, EXT - 1, 0) - pltpu.roll(here, 1, 0)) * 0.5
                grad_y = (east[tile] - west[tile]) * 0.5
                lean = sigma * press_z
                wide[k, tile] = wide[k, tile] - step * (grad_x - terrain[0, tile] * lean)
                wide[8 + k, tile] = wide[8 + k, tile] - step * (grad_y - terrain[1, tile] * lean)
                wide[16 + k, tile] = wide[16 + k, tile] - 0.5 * press_z
        for k in range(L):
            up, low = min(k + 1, L - 1), max(k - 1, 0)
            sigma = 1.0 - (k + 0.5) / L
            north = next_col(wide[8 + k, 0], wide[8 + k, 1], lane)
            south = prev_col(wide[8 + k, 0], wide[8 + k, 1], lane)
            for tile in range(2):
                wind = wide[k, tile]
                flat = pltpu.roll(wind, EXT - 1, 0) - pltpu.roll(wind, 1, 0) + north[tile] - south[tile]
                slope = terrain[0, tile] * (wide[up, tile] - wide[low, tile])
                slope = slope + terrain[1, tile] * (wide[8 + up, tile] - wide[8 + low, tile])
                rise = wide[16 + up, tile] - wide[16 + low, tile]
                spread = 0.5 * (flat + terrain[2, tile] * (rise - sigma * slope))
                wide[24 + k, tile] = wide[24 + k, tile] - terrain[3, tile] * spread
        return carry

    lax.fori_loop(0, SUB, substep, 0)
    for plane in range(4 * L):
        out[plane * ROWS : plane * ROWS + ROWS, :] = wide[plane, 0, HALO : HALO + ROWS, :]


def spread_kernel(got, placement, slots):
    nest = jnp.minimum(lax.axis_index("gx"), NESTS - 1)
    ox, oy = placement[nest, 0], placement[nest, 1]

    def rows_of(first):
        parts = []
        for a in range(2):
            start = ((first + a) // ROWS) * SLOT + a * 24
            parts.append(got[pl.ds(pl.multiple_of(start, 8), 24), :])
        return jnp.concatenate(parts, 0)

    west, east = rows_of(ox), rows_of(ox + EAST)
    lane = iota((X_ROWS, LANES), 1)
    fine = iota((16, LANES), 1) % ROWS
    for q in range(8):
        shift = (oy + (LANES * q) // R) % LANES
        left = pltpu.roll(west, (LANES - shift) % LANES, 1)
        right = pltpu.roll(east, (LANES + 64 - shift) % LANES, 1)
        slots[q * SLOT : q * SLOT + X_ROWS, :] = jnp.where(lane < 64, left, right)
        start = ox + (ROWS * q) // R
        low = start // ROWS
        high = jnp.minimum(low + 1, 7)
        near = got[pl.ds(pl.multiple_of(low * SLOT + X_ROWS, 8), 16), :]
        far = got[pl.ds(pl.multiple_of(high * SLOT + X_ROWS, 8), 16), :]
        slots[q * SLOT + X_ROWS : q * SLOT + SLOT, :] = jnp.where(fine >= start % ROWS, near, far)


def merge_kernel(got, placement, across, south, north):
    nest = jnp.minimum(lax.axis_index("gx"), NESTS - 1)
    oy = placement[nest, 1]
    start = oy + (LANES * lax.axis_index("gy")) // R
    low = start // LANES
    high = jnp.minimum(low + 1, 7)
    near = got[pl.ds(pl.multiple_of(low * SLOT, 8), X_ROWS), :]
    far = got[pl.ds(pl.multiple_of(high * SLOT, 8), X_ROWS), :]
    lane = iota((X_ROWS, LANES), 1) % 64
    across[...] = jnp.where(lane < LANES * (low + 1) - start, near, far)

    def columns(col):
        return got[pl.ds(pl.multiple_of((col // LANES) * SLOT + X_ROWS, 8), 16), :]

    which = iota((16, LANES), 0) % 3
    south[...] = jnp.where(which == 0, columns(oy), columns(oy + 1))
    top = oy + NORTH
    north[...] = jnp.where(which == 0, columns(top), jnp.where(which == 1, columns(top + 1), columns(top + 2)))


def third(value):
    return (value * 171) >> 9


def relax_kernel(moved, west, east, south, north, placement, zones, out):
    group = lax.axis_index("nest")
    gx = lax.axis_index("gx")
    gy = lax.axis_index("gy")
    nest = jnp.minimum(group, NESTS - 1)
    ox = placement[nest, 0]
    last_x, last_y = lax.axis_size("gx") - 1, lax.axis_size("gy") - 1
    source = jnp.where(gx == 0, west[...], east[...])
    lane = iota((X_ROWS, LANES), 1)
    phase = (LANES * gy) % R
    index = third(lane + phase) + jnp.where(gx == 0, 0, 64)
    across = jnp.take_along_axis(source, index, axis=1)

    big_row, big_lane = iota((LANES, LANES), 0), iota((LANES, LANES), 1)
    parent_row = (ox + third(ROWS * gx + big_row % ROWS)) % ROWS
    pick = ((big_row // ROWS == big_lane // ROWS) & (big_lane % ROWS == parent_row)).astype(F32)

    row, col = iota((ROWS, LANES), 0), iota((ROWS, LANES), 1)
    row_pos, col_pos = (row + ROWS * gx).astype(F32), (col + LANES * gy).astype(F32)
    weight = jnp.zeros((ROWS, LANES), F32)
    for edge, dist in enumerate((row_pos, N_X - 1 - row_pos, col_pos, N_Y - 1 - col_pos)):
        width = zones[nest, edge].astype(F32)
        weight = jnp.maximum(weight, jnp.maximum((width - dist) / width, 0.0))
    weight = jnp.where(group < NESTS, weight, 0.0)
    in_x = ((gx == 0) & (row < W_MAX)) | ((gx == last_x) & (row >= ROWS - W_MAX))
    split = jnp.where(gx == 0, 3, ROWS - 2)

    for c, field in enumerate((0, 1, 3)):
        s0, s1 = south[3 * c : 3 * c + 1, :], south[3 * c + 1 : 3 * c + 2, :]
        n0, n1, n2 = (north[3 * c + b : 3 * c + b + 1, :] for b in range(3))
        none = jnp.zeros((1, LANES), F32)
        table = jnp.concatenate(
            [s0, s0, s0, s1, s1, none, none, none, jnp.zeros((112, LANES), F32), none, none, none, n0, n1, n1, n1, n2], 0
        )
        along = lax.dot_general(pick, table, (((1,), (1,)), ((), ())), precision=HIGH, preferred_element_type=F32)
        for k in range(L):
            plane = c * L + k
            line0 = jnp.broadcast_to(across[plane : plane + 1, :], (ROWS, LANES))
            line1 = jnp.broadcast_to(across[24 + plane : 25 + plane, :], (ROWS, LANES))
            target = jnp.where(in_x, jnp.where(row < split, line0, line1), along[k * ROWS : k * ROWS + ROWS, :])
            at = (field * L + k) * ROWS
            value = moved[at : at + ROWS, :]
            out[at : at + ROWS, :] = value + weight * (target - value)
    out[2 * L * ROWS : 3 * L * ROWS, :] = moved[2 * L * ROWS : 3 * L * ROWS, :]


def call(kernel, specs, outs, scratch=()):
    many = tuple(jax.ShapeDtypeStruct(shape, F32) for shape in outs)
    return pl.pallas_call(
        kernel,
        in_specs=list(specs),
        out_specs=tuple(VMEM_SPEC for _ in outs),
        out_shape=many,
        scratch_shapes=list(scratch),
    )


def local(state, metric, placement, zones):
    flat = state.reshape(4 * L * ROWS, LANES)
    ground = metric.reshape(3 * ROWS, LANES)
    V, S = VMEM_SPEC, SMEM_SPEC
    size = lax.axis_size("gx")
    up_pairs = [(i, i + 1) for i in range(size - 1)]
    down_pairs = [(i + 1, i) for i in range(size - 1)]

    slots, left, right = call(pack_kernel, (V, V, S), [(8 * SLOT, LANES), (48, LANES), (48, LANES)])(
        flat, ground, placement
    )
    first = lax.all_to_all(slots.reshape(8, SLOT, LANES), "gx", 0, 0).reshape(8 * SLOT, LANES)
    from_left = lax.ppermute(right, "gy", up_pairs)
    from_right = lax.ppermute(left, "gy", down_pairs)
    ext = PLANES * 8 + 48
    to_up, to_down = call(join_kernel, (V, V, V, V), [(ext, LANES)] * 2)(flat, ground, from_left, from_right)
    from_up = lax.ppermute(to_down, "gx", up_pairs)
    from_down = lax.ppermute(to_up, "gx", down_pairs)
    (second,) = call(spread_kernel, (V, S), [(8 * SLOT, LANES)])(first, placement)
    arrived = lax.all_to_all(second.reshape(8, SLOT, LANES), "gy", 0, 0).reshape(8 * SLOT, LANES)
    (moved,) = call(
        advance_kernel,
        (V,) * 6,
        [(4 * L * ROWS, LANES)],
        [pltpu.VMEM((4 * L, 2, EXT, LANES), F32), pltpu.VMEM((4, 2, EXT, LANES), F32)],
    )(flat, ground, from_left, from_right, from_up, from_down)
    across, south, north = call(merge_kernel, (V, S), [(X_ROWS, LANES), (16, LANES), (16, LANES)])(arrived, placement)
    axes = ("nest", "gx", "gy")

    def send(value, place):
        pairs = []
        for n in range(NESTS):
            for q in range(8):
                x, y = place(q)
                pairs.append(((NESTS * 8 + n) * 8 + q, (n * 8 + x) * 8 + y))
        return lax.ppermute(value, axes, pairs)

    west = send(across, lambda q: (0, q))
    east = send(across, lambda q: (7, q))
    bottom = send(south, lambda q: (q, 0))
    top = send(north, lambda q: (q, 7))
    (result,) = call(relax_kernel, (V,) * 5 + (S, S), [(4 * L * ROWS, LANES)])(
        moved, west, east, bottom, top, placement, zones
    )
    return result.reshape(state.shape)


def solution(mesh):
    return jax.shard_map(
        local,
        mesh=mesh,
        in_specs=(P("nest", None, None, "gx", "gy"), P("nest", None, "gx", "gy"), P(), P()),
        out_specs=P("nest", None, None, "gx", "gy"),
        check_vma=False,
    )
```

```python
import jax
import jax.numpy as jnp
from jax import lax
from jax.experimental import pallas as pl
from jax.experimental.pallas import tpu as pltpu
from jax.sharding import PartitionSpec as P


SUB = 4
R = 3
W_MAX = 5
L = 8
NESTS = 7
HALO = 8
ROWS = 16
LANES = 128
PLANES = 4 * L + 3
SLOT = 64
FINE = 32
X_ROWS = 48
THREE = 24
N_X = 128
N_Y = 1024
EAST = (N_X - 1) // R - 1
NORTH = (N_Y - 1) // R - 2
F32 = jnp.float32
HIGH = lax.Precision.HIGHEST

SEAT = (4, 1, 7, 2, 6, 3, 5)

SEAT = (4, 1, 7, 2, 6, 3, 5)
SPARE = 0

VMEM_SPEC = pl.BlockSpec(memory_space=pltpu.VMEM)
SMEM_SPEC = pl.BlockSpec(memory_space=pltpu.SMEM)


def iota(shape, dim):
    return lax.broadcasted_iota(jnp.int32, shape, dim)


def plane_row(state, metric, plane, row, count):
    if plane < 4 * L:
        return state[plane * ROWS + row : plane * ROWS + row + count, :]
    start = (plane - 4 * L) * ROWS + row
    return metric[start : start + count, :]


def select_kernel(state, placement, slots, fields, store, sems, out_sems):
    gx = lax.axis_index("gx")
    gy = lax.axis_index("gy")
    loads = []
    for t, field in enumerate((0, 1, 3)):
        rows = pl.ds(field * L * ROWS, L * ROWS)
        loads.append(pltpu.make_async_copy(state.at[rows], fields.at[pl.ds(t * L * ROWS, L * ROWS)], sems.at[t]))
        loads[-1].start()
    rows_n = iota((THREE, LANES), 0)
    first = jnp.zeros((THREE, LANES), jnp.int32)
    bases = []
    for n in range(NESTS):
        low = placement[0, n] - ROWS * gx
        bases.append(jnp.where((low >= -1) & (low < ROWS), low, low + EAST))
        low = placement[1, n] - LANES * gy
        base = jnp.where((low >= -1) & (low < LANES), low, low + NORTH)
        first = jnp.where((rows_n >= 3 * n) & (rows_n < 3 * n + 3), base + rows_n - 3 * n, first)
    pick = (iota((THREE, LANES), 1) == first).astype(F32)
    for t in range(3):
        loads[t].wait()
        start = t * L * ROWS
        cols = lax.dot_general(
            pick, fields[start : start + 128, :], (((1,), (1,)), ((), ())), precision=HIGH, preferred_element_type=F32
        )
        for n in range(NESTS):
            at = SEAT[n] * SLOT
            for a in range(2):
                row = jnp.clip(bases[n] + a, 0, ROWS - 1)
                out = at + a * THREE + t * L
                store[out : out + L, :] = fields[pl.ds(start + row, L, stride=ROWS), :]
            store[at + X_ROWS + 3 * t : at + X_ROWS + 3 * t + 3, :] = cols[3 * n : 3 * n + 3, :]
    for n in range(8):
        part = pl.ds(n * SLOT, SLOT)
        if n == SPARE:
            store[part, :] = jnp.zeros((SLOT, LANES), F32)
        else:
            store[n * SLOT + X_ROWS + 9 : n * SLOT + SLOT, :] = jnp.zeros((7, LANES), F32)
    whole_copy = pltpu.make_async_copy(store, slots, out_sems.at[0])
    whole_copy.start()
    whole_copy.wait()


def edge_kernel(state, metric, up, down):
    for plane in range(PLANES):
        up[plane * 8 : plane * 8 + 8, :] = plane_row(state, metric, plane, 0, 8)
        down[plane * 8 : plane * 8 + 8, :] = plane_row(state, metric, plane, 8, 8)


def strip(state, metric, from_up, from_down, plane, rt):
    if rt == 0:
        return from_up[plane * 8 : plane * 8 + 8, :]
    if rt == 3:
        return from_down[plane * 8 : plane * 8 + 8, :]
    return plane_row(state, metric, plane, (rt - 1) * 8, 8)


def pack_kernel(state, metric, from_up, from_down, left, right):
    lane = iota((8, LANES), 1) // 8
    for rt in range(4):
        for group in range(3):
            left_sum = jnp.zeros((8, LANES), F32)
            right_sum = jnp.zeros((8, LANES), F32)
            for s in range(16):
                plane = group * 16 + s
                if plane >= PLANES:
                    break
                value = strip(state, metric, from_up, from_down, plane, rt)
                left_sum = jnp.where(lane == s, pltpu.roll(value, 8 * s, 1) if s else value, left_sum)
                shift = (8 * s + 8) % LANES
                right_sum = jnp.where(lane == s, pltpu.roll(value, shift, 1) if shift else value, right_sum)
            at = (rt * 3 + group) * 8
            left[at : at + 8, :] = left_sum
            right[at : at + 8, :] = right_sum


def next_col(centre, halo, lane):
    edge = lane == 0
    return (
        pltpu.roll(jnp.where(edge, halo, centre), LANES - 1, 1),
        pltpu.roll(jnp.where(edge, centre, halo), LANES - 1, 1),
    )


def prev_col(centre, halo, lane):
    edge = lane == LANES - 1
    return pltpu.roll(jnp.where(edge, halo, centre), 1, 1), pltpu.roll(jnp.where(edge, centre, halo), 1, 1)


EXT = ROWS + 2 * HALO


def advance_kernel(state, metric, from_up, from_down, from_left, from_right, out, wide, terrain):
    gx = lax.axis_index("gx")
    gy = lax.axis_index("gy")
    lane8 = iota((8, LANES), 1)
    for plane in range(PLANES):
        group, s = divmod(plane, 16)
        for rt in range(4):
            at = (rt * 3 + group) * 8
            right_part = pltpu.roll(from_right[at : at + 8, :], (LANES - 8 * s) % LANES, 1)
            left_part = pltpu.roll(from_left[at : at + 8, :], (120 - 8 * s) % LANES, 1)
            halo = jnp.where(lane8 < 8, right_part, jnp.where(lane8 >= 120, left_part, 0.0))
            centre = strip(state, metric, from_up, from_down, plane, rt)
            if plane < 4 * L:
                wide[plane, 0, rt * 8 : rt * 8 + 8, :] = centre
                wide[plane, 1, rt * 8 : rt * 8 + 8, :] = halo
            else:
                terrain[plane - 4 * L, 0, rt * 8 : rt * 8 + 8, :] = centre
                terrain[plane - 4 * L, 1, rt * 8 : rt * 8 + 8, :] = halo

    row = iota((EXT, LANES), 0) + ROWS * gx - HALO
    lane = iota((EXT, LANES), 1)
    row_in = (row >= 0) & (row < N_X)
    last = lax.axis_size("gy") - 1
    halo_in = row_in & (((lane < 8) & (gy < last)) | ((lane >= 120) & (gy > 0)))
    for tile, inside in ((0, row_in), (1, halo_in)):
        inverse = 1.0 / jnp.where(inside, terrain[2, tile], 1.0)
        terrain[2, tile] = inverse
        terrain[3, tile] = jnp.where(inside, 0.5, 0.0)

    def substep(_, carry):
        for k in range(L):
            up, low = min(k + 1, L - 1), max(k - 1, 0)
            sigma = 1.0 - (k + 0.5) / L
            centre, halo = wide[24 + k, 0], wide[24 + k, 1]
            east = next_col(centre, halo, lane)
            west = prev_col(centre, halo, lane)
            for tile in range(2):
                here = (centre, halo)[tile]
                step = terrain[3, tile]
                press_z = (wide[24 + up, tile] - wide[24 + low, tile]) * (0.5 * terrain[2, tile])
                grad_x = (pltpu.roll(here, EXT - 1, 0) - pltpu.roll(here, 1, 0)) * 0.5
                grad_y = (east[tile] - west[tile]) * 0.5
                lean = sigma * press_z
                wide[k, tile] = wide[k, tile] - step * (grad_x - terrain[0, tile] * lean)
                wide[8 + k, tile] = wide[8 + k, tile] - step * (grad_y - terrain[1, tile] * lean)
                wide[16 + k, tile] = wide[16 + k, tile] - 0.5 * press_z
        for k in range(L):
            up, low = min(k + 1, L - 1), max(k - 1, 0)
            sigma = 1.0 - (k + 0.5) / L
            north = next_col(wide[8 + k, 0], wide[8 + k, 1], lane)
            south = prev_col(wide[8 + k, 0], wide[8 + k, 1], lane)
            for tile in range(2):
                wind = wide[k, tile]
                flat = pltpu.roll(wind, EXT - 1, 0) - pltpu.roll(wind, 1, 0) + north[tile] - south[tile]
                slope = terrain[0, tile] * (wide[up, tile] - wide[low, tile])
                slope = slope + terrain[1, tile] * (wide[8 + up, tile] - wide[8 + low, tile])
                rise = wide[16 + up, tile] - wide[16 + low, tile]
                spread = 0.5 * (flat + terrain[2, tile] * (rise - sigma * slope))
                wide[24 + k, tile] = wide[24 + k, tile] - terrain[3, tile] * spread
        return carry

    lax.fori_loop(0, SUB, substep, 0)
    for plane in range(4 * L):
        out[plane * ROWS : plane * ROWS + ROWS, :] = wide[plane, 0, HALO : HALO + ROWS, :]


def seated(seat):
    nest = 0
    for n in range(1, NESTS):
        nest = jnp.where(seat == SEAT[n], n, nest)
    return nest


def spread_kernel(got, placement, slots):
    gx = lax.axis_index("gx")
    nest = seated(lax.axis_index("gy"))
    ox, oy = placement[0, nest], placement[1, nest]
    lane = iota((THREE, LANES), 1)

    def line(col, b, c):
        return got[pl.ds((col // LANES) * SLOT + X_ROWS + 3 * c + b, 1), :]

    south = [[line(oy + b, b, c) for c in range(3)] for b in range(2)]
    north = [[line(oy + NORTH + b, b, c) for c in range(3)] for b in range(3)]
    even = jnp.concatenate(south[0] + north[0] + [north[2][0], north[2][2]], 0)
    odd = jnp.concatenate(south[1] + north[1] + [north[2][1], north[2][2]], 0)
    half = iota((8, LANES), 1) % ROWS < 8
    for q in range(8):
        start = oy + (LANES * q) // R
        low = start // LANES
        high = jnp.minimum(low + 1, 7)
        shift = start % LANES
        parts = []
        for a in range(2):
            near = got[pl.ds(pl.multiple_of(low * SLOT + a * THREE, 8), THREE), :]
            far = got[pl.ds(pl.multiple_of(high * SLOT + a * THREE, 8), THREE), :]
            parts.append(pltpu.roll(jnp.where(lane >= shift, near, far), (LANES + 64 * a - shift) % LANES, 1))
        slots[q * FINE : q * FINE + THREE, :] = jnp.where(lane < 64, parts[0], parts[1])
        turn = ROWS * gx - ox - (ROWS * q) // R + 4 * LANES
        slots[q * FINE + THREE : q * FINE + FINE, :] = jnp.where(
            half, pltpu.roll(even, turn % LANES, 1), pltpu.roll(odd, (turn + 8) % LANES, 1)
        )


def merge_kernel(got, placement, west, east, along):
    nest = seated(lax.axis_index("gy"))
    ox = placement[0, nest]
    lane = iota((THREE, LANES), 1)

    def rows(row):
        return got[pl.ds(pl.multiple_of((row // ROWS) * FINE, 8), THREE), :]

    west[...] = jnp.where(lane < 64, rows(ox), rows(ox + 1))
    east[...] = jnp.where(lane < 64, rows(ox + EAST), rows(ox + EAST + 1))
    start = ox + (ROWS * lax.axis_index("gx")) // R
    low = start // ROWS
    high = jnp.minimum(low + 1, 7)
    near = got[pl.ds(pl.multiple_of(low * FINE + THREE, 8), 8), :]
    far = got[pl.ds(pl.multiple_of(high * FINE + THREE, 8), 8), :]
    along[...] = jnp.where(iota((8, LANES), 1) % 8 < ROWS * (low + 1) - start, near, far)


def third(value):
    return (value * 171) >> 9


def relax_kernel(moved, west, east, south, north, placement, zones, out, store, sems):
    group = lax.axis_index("nest")
    gx = lax.axis_index("gx")
    gy = lax.axis_index("gy")
    nest = jnp.minimum(group, NESTS - 1)
    last_x = lax.axis_size("gx") - 1
    size = L * ROWS
    copies = [
        pltpu.make_async_copy((moved if f == 2 else store).at[pl.ds(f * size, size)], out.at[pl.ds(f * size, size)], sems.at[f])
        for f in range(4)
    ]
    copies[2].start()
    source = jnp.where(gx == 0, west[...], east[...])
    index = third(iota((THREE, LANES), 1) + (LANES * gy) % R)
    lines = [jnp.take_along_axis(source, index + 64 * a, axis=1) for a in range(2)]

    big_row, big_lane = iota((LANES, LANES), 0), iota((LANES, LANES), 1)
    need = third(big_row % ROWS + (ROWS * gx) % R)
    pick = ((big_row // ROWS == big_lane // ROWS) & (big_lane % 8 == need)).astype(F32)

    row, col = iota((ROWS, LANES), 0), iota((ROWS, LANES), 1)
    row_pos, col_pos = (row + ROWS * gx).astype(F32), (col + LANES * gy).astype(F32)
    weight = jnp.zeros((ROWS, LANES), F32)
    for edge, dist in enumerate((row_pos, N_X - 1 - row_pos, col_pos, N_Y - 1 - col_pos)):
        width = zones[edge, nest].astype(F32)
        weight = jnp.maximum(weight, jnp.maximum((width - dist) / width, 0.0))
    weight = jnp.where(group < NESTS, weight, 0.0)
    in_x = ((gx == 0) & (row < W_MAX)) | ((gx == last_x) & (row >= ROWS - W_MAX))
    split = jnp.where(gx == 0, 3, ROWS - 2)

    lane8, row8 = iota((8, LANES), 1), iota((8, LANES), 0)
    first_half = lane8 % ROWS < 8
    for c, field in enumerate((0, 1, 3)):
        pair = jnp.broadcast_to(south[c : c + 1, :], (8, LANES))
        low = jnp.where(first_half == (row8 < 3), pair, 0.0)
        low = jnp.where(row8 < W_MAX, low, 0.0)
        pair = jnp.broadcast_to(north[3 + c : 4 + c, :], (8, LANES))
        last = jnp.broadcast_to(north[(6, 6, 7)[c] : (7, 7, 8)[c], :], (8, LANES))
        last = jnp.where(first_half == (c != 1), last, 0.0)
        high = jnp.where(first_half == (row8 < 4), pair, 0.0)
        high = jnp.where(row8 == 7, last, jnp.where(row8 >= 3, high, 0.0))
        table = jnp.concatenate([low, jnp.zeros((112, LANES), F32), high], 0)
        along = lax.dot_general(pick, table, (((1,), (1,)), ((), ())), precision=HIGH, preferred_element_type=F32)
        for k in range(L):
            plane = c * L + k
            line0 = jnp.broadcast_to(lines[0][plane : plane + 1, :], (ROWS, LANES))
            line1 = jnp.broadcast_to(lines[1][plane : plane + 1, :], (ROWS, LANES))
            target = jnp.where(in_x, jnp.where(row < split, line0, line1), along[k * ROWS : k * ROWS + ROWS, :])
            at = (field * L + k) * ROWS
            value = moved[at : at + ROWS, :]
            store[at : at + ROWS, :] = value + weight * (target - value)
        copies[field].start()
    for f in range(4):
        copies[f].wait()


ANY_SPEC = pl.BlockSpec(memory_space=pl.ANY)


def call(kernel, specs, outs, scratch=(), near=True):
    many = tuple(pltpu.VMEM(shape, F32) if near else jax.ShapeDtypeStruct(shape, F32) for shape in outs)
    run = pl.pallas_call(
        kernel,
        in_specs=list(specs),
        out_specs=tuple(VMEM_SPEC if near else ANY_SPEC for _ in outs),
        out_shape=many,
        scratch_shapes=list(scratch),
    )

    def placed(*args):
        return run(*(pltpu.with_memory_space_constraint(a, pltpu.VMEM) if s is VMEM_SPEC else a for a, s in zip(args, specs)))

    return placed


def local(state, metric, placement, zones):
    return whole(state, metric, placement.T, zones.T)


def whole(state, metric, placement, zones):
    flat = state.reshape(4 * L * ROWS, LANES)
    ground = metric.reshape(3 * ROWS, LANES)
    V, S, A = VMEM_SPEC, SMEM_SPEC, ANY_SPEC
    size = lax.axis_size("gx")
    up_pairs = [(i, i + 1) for i in range(size - 1)]
    down_pairs = [(i + 1, i) for i in range(size - 1)]
    axes = ("nest", "gx", "gy")
    DMA = pltpu.SemaphoreType.DMA

    (slots,) = call(
        select_kernel,
        (A, S),
        [(8 * SLOT, LANES)],
        [pltpu.VMEM((3 * L * ROWS, LANES), F32), pltpu.VMEM((8 * SLOT, LANES), F32), DMA((3,)), DMA((1,))],
        near=False,
    )(flat, placement)
    first = lax.all_to_all(slots.reshape(8, SLOT, LANES), "gy", 0, 0).reshape(8 * SLOT, LANES)
    to_up, to_down = call(edge_kernel, (V, V), [(PLANES * 8, LANES)] * 2)(flat, ground)
    from_up = lax.ppermute(to_down, "gx", up_pairs)
    from_down = lax.ppermute(to_up, "gx", down_pairs)
    (second,) = call(spread_kernel, (V, S), [(8 * FINE, LANES)])(first, placement)
    arrived = lax.all_to_all(second.reshape(8, FINE, LANES), "gx", 0, 0).reshape(8 * FINE, LANES)
    left, right = call(pack_kernel, (V,) * 4, [(96, LANES)] * 2)(flat, ground, from_up, from_down)
    from_left = lax.ppermute(right, "gy", up_pairs)
    from_right = lax.ppermute(left, "gy", down_pairs)
    across, beyond, along = call(merge_kernel, (V, S), [(THREE, LANES), (THREE, LANES), (8, LANES)])(arrived, placement)

    def send(value, place):
        pairs = []
        for n in range(NESTS):
            for q in range(8):
                x, y = place(q)
                pairs.append(((NESTS * 8 + q) * 8 + SEAT[n], (n * 8 + x) * 8 + y))
        return lax.ppermute(value, axes, pairs)

    west = send(across, lambda q: (0, q))
    east = send(beyond, lambda q: (7, q))
    top = send(along, lambda q: (q, 7))
    bottom = send(along, lambda q: (q, 0))
    (moved,) = call(
        advance_kernel,
        (V,) * 6,
        [(4 * L * ROWS, LANES)],
        [pltpu.VMEM((4 * L, 2, EXT, LANES), F32), pltpu.VMEM((4, 2, EXT, LANES), F32)],
    )(flat, ground, from_up, from_down, from_left, from_right)
    (result,) = call(
        relax_kernel,
        (V,) * 5 + (S, S),
        [(4 * L * ROWS, LANES)],
        [pltpu.VMEM((4 * L * ROWS, LANES), F32), DMA((4,))],
        near=False,
    )(moved, west, east, bottom, top, placement, zones)
    return result.reshape(state.shape)


def solution(mesh):
    return jax.shard_map(
        local,
        mesh=mesh,
        in_specs=(P("nest", None, None, "gx", "gy"), P("nest", None, "gx", "gy"), P(), P()),
        out_specs=P("nest", None, None, "gx", "gy"),
        check_vma=False,
    )
```

```python
import jax
import jax.numpy as jnp
from jax import lax
from jax.experimental import pallas as pl
from jax.experimental.pallas import tpu as pltpu
from jax.sharding import PartitionSpec as P


SUB = 4
R = 3
W_MAX = 5
L = 8
NESTS = 7
HALO = 8
ROWS = 16
LANES = 128
PLANES = 4 * L + 3
SLOT = 64
FINE = 32
X_ROWS = 48
THREE = 24
N_X = 128
N_Y = 1024
EAST = (N_X - 1) // R - 1
NORTH = (N_Y - 1) // R - 2
F32 = jnp.float32
HIGH = lax.Precision.HIGHEST

SEAT = (4, 1, 7, 2, 6, 3, 5)

SEAT = (6, 3, 7, 2, 5, 1, 4)
SPARE = 0


def ring(a, b):
    return min((a - b) % 8, (b - a) % 8)


def pieces_of(n):
    far = sorted(range(8), key=lambda q: -ring(4 + SEAT[n] // 2, 4 * (n % 2) + q // 2))
    near = sorted(range(8), key=lambda g: max(ring(g, 0), ring(g, 7)))
    return tuple(q for _, q in sorted(zip(near, far)))


PIECE = tuple(pieces_of(n) for n in range(NESTS))

VMEM_SPEC = pl.BlockSpec(memory_space=pltpu.VMEM)


def iota(shape, dim):
    return lax.broadcasted_iota(jnp.int32, shape, dim)


def plane_row(state, metric, plane, row, count):
    if plane < 4 * L:
        return state[plane * ROWS + row : plane * ROWS + row + count, :]
    start = (plane - 4 * L) * ROWS + row
    return metric[start : start + count, :]


def select_kernel(state, where, slots, info, fields, store, placement, sems, out_sems):
    gx = lax.axis_index("gx")
    gy = lax.axis_index("gy")
    ask = pltpu.make_async_copy(where, placement, sems.at[3])
    ask.start()
    loads = []
    for t, field in enumerate((0, 1, 3)):
        rows = pl.ds(field * L * ROWS, L * ROWS)
        loads.append(pltpu.make_async_copy(state.at[rows], fields.at[pl.ds(t * L * ROWS, L * ROWS)], sems.at[t]))
        loads[-1].start()
    ask.wait()
    rows_n = iota((THREE, LANES), 0)
    first = jnp.zeros((THREE, LANES), jnp.int32)
    bases = []
    for n in range(NESTS):
        low = placement[0, n] - ROWS * gx
        bases.append(jnp.where((low >= -1) & (low < ROWS), low, low + EAST))
        low = placement[1, n] - LANES * gy
        base = jnp.where((low >= -1) & (low < LANES), low, low + NORTH)
        first = jnp.where((rows_n >= 3 * n) & (rows_n < 3 * n + 3), base + rows_n - 3 * n, first)
    pick = (iota((THREE, LANES), 1) == first).astype(F32)
    store[SPARE] = jnp.zeros((SLOT, LANES), F32)
    for t in range(3):
        loads[t].wait()
        start = t * L * ROWS
        for n in range(NESTS):
            for a in range(2):
                row = jnp.clip(bases[n] + a, 0, ROWS - 1)
                out = a * THREE + t * L
                store[SEAT[n], out : out + L, :] = fields[pl.ds(start + row, L, stride=ROWS), :]
    lower = pltpu.make_async_copy(store.at[:, 0:X_ROWS], slots.at[:, 0:X_ROWS], out_sems.at[0])
    lower.start()
    line, spot = iota((8, LANES), 0), iota((8, LANES), 1)
    kept = jnp.zeros((8, LANES), F32)
    for n in range(NESTS):
        pair = jnp.where(line == 0, placement[0, n], placement[1, n]).astype(F32)
        kept = jnp.where(spot == n, pair, kept)
    info[...] = kept
    for t in range(3):
        start = t * L * ROWS
        cols = lax.dot_general(
            pick, fields[start : start + 128, :], (((1,), (1,)), ((), ())), precision=HIGH, preferred_element_type=F32
        )
        for n in range(NESTS):
            store[SEAT[n], X_ROWS + 3 * t : X_ROWS + 3 * t + 3, :] = cols[3 * n : 3 * n + 3, :]
    for n in range(NESTS):
        store[SEAT[n], X_ROWS + 9 : SLOT, :] = jnp.zeros((7, LANES), F32)
    upper = pltpu.make_async_copy(store.at[:, X_ROWS:SLOT], slots.at[:, X_ROWS:SLOT], out_sems.at[1])
    upper.start()
    lower.wait()
    upper.wait()


def edge_kernel(state, metric, up, down):
    for plane in range(PLANES):
        up[plane * 8 : plane * 8 + 8, :] = plane_row(state, metric, plane, 0, 8)
        down[plane * 8 : plane * 8 + 8, :] = plane_row(state, metric, plane, 8, 8)


def fetch_kernel(state, metric, from_up, from_down, copy, ground, above, below, sems):
    pairs = ((state, copy), (metric, ground), (from_up, above), (from_down, below))
    copies = [pltpu.make_async_copy(a, b, sems.at[i]) for i, (a, b) in enumerate(pairs)]
    for one in copies:
        one.start()
    for one in copies:
        one.wait()


def strip(state, metric, from_up, from_down, plane, rt):
    if rt == 0:
        return from_up[plane * 8 : plane * 8 + 8, :]
    if rt == 3:
        return from_down[plane * 8 : plane * 8 + 8, :]
    return plane_row(state, metric, plane, (rt - 1) * 8, 8)


def pack_kernel(state, metric, from_up, from_down, left, right):
    lane = iota((8, LANES), 1) // 8
    for rt in range(4):
        for group in range(3):
            left_sum = jnp.zeros((8, LANES), F32)
            right_sum = jnp.zeros((8, LANES), F32)
            for s in range(16):
                plane = group * 16 + s
                if plane >= PLANES:
                    break
                value = strip(state, metric, from_up, from_down, plane, rt)
                left_sum = jnp.where(lane == s, pltpu.roll(value, 8 * s, 1) if s else value, left_sum)
                shift = (8 * s + 8) % LANES
                right_sum = jnp.where(lane == s, pltpu.roll(value, shift, 1) if shift else value, right_sum)
            at = (rt * 3 + group) * 8
            left[at : at + 8, :] = left_sum
            right[at : at + 8, :] = right_sum


def next_col(centre, halo, lane):
    edge = lane == 0
    return (
        pltpu.roll(jnp.where(edge, halo, centre), LANES - 1, 1),
        pltpu.roll(jnp.where(edge, centre, halo), LANES - 1, 1),
    )


def prev_col(centre, halo, lane):
    edge = lane == LANES - 1
    return pltpu.roll(jnp.where(edge, halo, centre), 1, 1), pltpu.roll(jnp.where(edge, centre, halo), 1, 1)


EXT = ROWS + 2 * HALO


def advance_kernel(state, metric, from_up, from_down, from_left, from_right, out, wide, terrain):
    gx = lax.axis_index("gx")
    gy = lax.axis_index("gy")
    lane8 = iota((8, LANES), 1)
    for plane in range(PLANES):
        group, s = divmod(plane, 16)
        for rt in range(4):
            at = (rt * 3 + group) * 8
            right_part = pltpu.roll(from_right[at : at + 8, :], (LANES - 8 * s) % LANES, 1)
            left_part = pltpu.roll(from_left[at : at + 8, :], (120 - 8 * s) % LANES, 1)
            halo = jnp.where(lane8 < 8, right_part, jnp.where(lane8 >= 120, left_part, 0.0))
            centre = strip(state, metric, from_up, from_down, plane, rt)
            if plane < 4 * L:
                wide[plane, 0, rt * 8 : rt * 8 + 8, :] = centre
                wide[plane, 1, rt * 8 : rt * 8 + 8, :] = halo
            else:
                terrain[plane - 4 * L, 0, rt * 8 : rt * 8 + 8, :] = centre
                terrain[plane - 4 * L, 1, rt * 8 : rt * 8 + 8, :] = halo

    row = iota((EXT, LANES), 0) + ROWS * gx - HALO
    lane = iota((EXT, LANES), 1)
    row_in = (row >= 0) & (row < N_X)
    last = lax.axis_size("gy") - 1
    halo_in = row_in & (((lane < 8) & (gy < last)) | ((lane >= 120) & (gy > 0)))
    for tile, inside in ((0, row_in), (1, halo_in)):
        inverse = 1.0 / jnp.where(inside, terrain[2, tile], 1.0)
        terrain[2, tile] = inverse
        terrain[3, tile] = jnp.where(inside, 0.5, 0.0)

    def substep(_, carry):
        for k in range(L):
            up, low = min(k + 1, L - 1), max(k - 1, 0)
            sigma = 1.0 - (k + 0.5) / L
            centre, halo = wide[24 + k, 0], wide[24 + k, 1]
            east = next_col(centre, halo, lane)
            west = prev_col(centre, halo, lane)
            for tile in range(2):
                here = (centre, halo)[tile]
                step = terrain[3, tile]
                press_z = (wide[24 + up, tile] - wide[24 + low, tile]) * (0.5 * terrain[2, tile])
                grad_x = (pltpu.roll(here, EXT - 1, 0) - pltpu.roll(here, 1, 0)) * 0.5
                grad_y = (east[tile] - west[tile]) * 0.5
                lean = sigma * press_z
                wide[k, tile] = wide[k, tile] - step * (grad_x - terrain[0, tile] * lean)
                wide[8 + k, tile] = wide[8 + k, tile] - step * (grad_y - terrain[1, tile] * lean)
                wide[16 + k, tile] = wide[16 + k, tile] - 0.5 * press_z
        for k in range(L):
            up, low = min(k + 1, L - 1), max(k - 1, 0)
            sigma = 1.0 - (k + 0.5) / L
            north = next_col(wide[8 + k, 0], wide[8 + k, 1], lane)
            south = prev_col(wide[8 + k, 0], wide[8 + k, 1], lane)
            for tile in range(2):
                wind = wide[k, tile]
                flat = pltpu.roll(wind, EXT - 1, 0) - pltpu.roll(wind, 1, 0) + north[tile] - south[tile]
                slope = terrain[0, tile] * (wide[up, tile] - wide[low, tile])
                slope = slope + terrain[1, tile] * (wide[8 + up, tile] - wide[8 + low, tile])
                rise = wide[16 + up, tile] - wide[16 + low, tile]
                spread = 0.5 * (flat + terrain[2, tile] * (rise - sigma * slope))
                wide[24 + k, tile] = wide[24 + k, tile] - terrain[3, tile] * spread
        return carry

    lax.fori_loop(0, SUB, substep, 0)
    for plane in range(4 * L):
        out[plane * ROWS : plane * ROWS + ROWS, :] = wide[plane, 0, HALO : HALO + ROWS, :]


def seated(seat):
    nest = 0
    for n in range(1, NESTS):
        nest = jnp.where(seat == SEAT[n], n, nest)
    return nest


def corner(placement, nest):
    both = placement[...]
    mine = iota(both.shape, 1) == nest
    one = [jnp.sum(jnp.where(mine & (iota(both.shape, 0) == d), both, 0.0)) for d in range(2)]
    return one[0].astype(jnp.int32), one[1].astype(jnp.int32)


def spread_kernel(got, placement, slots, store, sems):
    gx = lax.axis_index("gx")
    nest = seated(lax.axis_index("gy"))
    ox, oy = corner(placement, nest)
    lane = iota((THREE, LANES), 1)

    def line(col, b, c):
        return got[pl.ds((col // LANES) * SLOT + X_ROWS + 3 * c + b, 1), :]

    south = [[line(oy + b, b, c) for c in range(3)] for b in range(2)]
    north = [[line(oy + NORTH + b, b, c) for c in range(3)] for b in range(3)]
    even = jnp.concatenate(south[0] + north[0] + [north[2][0], north[2][2]], 0)
    odd = jnp.concatenate(south[1] + north[1] + [north[2][1], north[2][2]], 0)
    half = iota((8, LANES), 1) % ROWS < 8
    copies = [
        pltpu.make_async_copy(store.at[pl.ds(h * 4 * FINE, 4 * FINE)], slots.at[pl.ds(h * 4 * FINE, 4 * FINE)], sems.at[h])
        for h in range(2)
    ]
    for g in range(8):
        reach = 0
        for n in range(NESTS):
            reach = jnp.where(nest == n, (LANES * PIECE[n][g]) // R, reach)
        start = oy + reach
        low = start // LANES
        high = jnp.minimum(low + 1, 7)
        shift = start % LANES
        parts = []
        for a in range(2):
            near = got[pl.ds(pl.multiple_of(low * SLOT + a * THREE, 8), THREE), :]
            far = got[pl.ds(pl.multiple_of(high * SLOT + a * THREE, 8), THREE), :]
            parts.append(pltpu.roll(jnp.where(lane >= shift, near, far), (LANES + 64 * a - shift) % LANES, 1))
        store[g * FINE : g * FINE + THREE, :] = jnp.where(lane < 64, parts[0], parts[1])
        turn = ROWS * gx - ox - (ROWS * g) // R + 4 * LANES
        store[g * FINE + THREE : g * FINE + FINE, :] = jnp.where(
            half, pltpu.roll(even, turn % LANES, 1), pltpu.roll(odd, (turn + 8) % LANES, 1)
        )
        if g % 4 == 3:
            copies[g // 4].start()
    for h in range(2):
        copies[h].wait()


def merge_kernel(got, placement, west, east, along):
    nest = seated(lax.axis_index("gy"))
    ox, _ = corner(placement, nest)
    lane = iota((THREE, LANES), 1)

    def rows(row):
        return got[pl.ds(pl.multiple_of((row // ROWS) * FINE, 8), THREE), :]

    west[...] = jnp.where(lane < 64, rows(ox), rows(ox + 1))
    east[...] = jnp.where(lane < 64, rows(ox + EAST), rows(ox + EAST + 1))
    start = ox + (ROWS * lax.axis_index("gx")) // R
    low = start // ROWS
    high = jnp.minimum(low + 1, 7)
    near = got[pl.ds(pl.multiple_of(low * FINE + THREE, 8), 8), :]
    far = got[pl.ds(pl.multiple_of(high * FINE + THREE, 8), 8), :]
    along[...] = jnp.where(iota((8, LANES), 1) % 8 < ROWS * (low + 1) - start, near, far)


def third(value):
    return (value * 171) >> 9


def relax_kernel(moved, west, east, south, north, zones, out, store, sems):
    group = lax.axis_index("nest")
    gx = lax.axis_index("gx")
    gy = lax.axis_index("gy")
    nest = jnp.minimum(group, NESTS - 1)
    last_x = lax.axis_size("gx") - 1
    size = L * ROWS
    copies = [
        pltpu.make_async_copy((moved if f == 2 else store).at[pl.ds(f * size, size)], out.at[pl.ds(f * size, size)], sems.at[f])
        for f in range(4)
    ]
    copies[2].start()
    source = jnp.where(gx == 0, west[...], east[...])
    index = third(iota((THREE, LANES), 1) + (LANES * gy) % R)
    lines = [jnp.take_along_axis(source, index + 64 * a, axis=1) for a in range(2)]

    big_row, big_lane = iota((LANES, LANES), 0), iota((LANES, LANES), 1)
    need = third(big_row % ROWS + (ROWS * gx) % R)
    pick = ((big_row // ROWS == big_lane // ROWS) & (big_lane % 8 == need)).astype(F32)

    row, col = iota((ROWS, LANES), 0), iota((ROWS, LANES), 1)
    row_pos, col_pos = (row + ROWS * gx).astype(F32), (col + LANES * gy).astype(F32)
    own = jnp.where(iota((4, NESTS), 1) == nest, zones[...].astype(F32), 0.0)
    widths = jnp.sum(own, axis=1, keepdims=True)
    weight = jnp.zeros((ROWS, LANES), F32)
    for edge, dist in enumerate((row_pos, N_X - 1 - row_pos, col_pos, N_Y - 1 - col_pos)):
        width = jnp.broadcast_to(widths[edge : edge + 1, :], (ROWS, LANES))
        weight = jnp.maximum(weight, jnp.maximum((width - dist) / width, 0.0))
    weight = jnp.where(group < NESTS, weight, 0.0)
    in_x = ((gx == 0) & (row < W_MAX)) | ((gx == last_x) & (row >= ROWS - W_MAX))
    split = jnp.where(gx == 0, 3, ROWS - 2)

    lane8, row8 = iota((8, LANES), 1), iota((8, LANES), 0)
    first_half = lane8 % ROWS < 8
    for c, field in enumerate((0, 1, 3)):
        pair = jnp.broadcast_to(south[c : c + 1, :], (8, LANES))
        low = jnp.where(first_half == (row8 < 3), pair, 0.0)
        low = jnp.where(row8 < W_MAX, low, 0.0)
        pair = jnp.broadcast_to(north[3 + c : 4 + c, :], (8, LANES))
        last = jnp.broadcast_to(north[(6, 6, 7)[c] : (7, 7, 8)[c], :], (8, LANES))
        last = jnp.where(first_half == (c != 1), last, 0.0)
        high = jnp.where(first_half == (row8 < 4), pair, 0.0)
        high = jnp.where(row8 == 7, last, jnp.where(row8 >= 3, high, 0.0))
        table = jnp.concatenate([low, jnp.zeros((112, LANES), F32), high], 0)
        along = lax.dot_general(pick, table, (((1,), (1,)), ((), ())), precision=HIGH, preferred_element_type=F32)
        for k in range(L):
            plane = c * L + k
            line0 = jnp.broadcast_to(lines[0][plane : plane + 1, :], (ROWS, LANES))
            line1 = jnp.broadcast_to(lines[1][plane : plane + 1, :], (ROWS, LANES))
            target = jnp.where(in_x, jnp.where(row < split, line0, line1), along[k * ROWS : k * ROWS + ROWS, :])
            at = (field * L + k) * ROWS
            value = moved[at : at + ROWS, :]
            store[at : at + ROWS, :] = value + weight * (target - value)
        copies[field].start()
    for f in range(4):
        copies[f].wait()


ANY_SPEC = pl.BlockSpec(memory_space=pl.ANY)


def call(kernel, specs, outs, scratch=(), near=True):
    places = near if isinstance(near, tuple) else (near,) * len(outs)
    many = tuple(pltpu.VMEM(shape, F32) if near_by else jax.ShapeDtypeStruct(shape, F32) for shape, near_by in zip(outs, places))
    run = pl.pallas_call(
        kernel,
        in_specs=list(specs),
        out_specs=tuple(VMEM_SPEC if near_by else ANY_SPEC for near_by in places),
        out_shape=many,
        scratch_shapes=list(scratch),
    )

    def placed(*args):
        return run(*(a if s is ANY_SPEC else pltpu.with_memory_space_constraint(a, s.memory_space) for a, s in zip(args, specs)))

    return placed


def local(state, metric, placement, zones):
    return whole(state, metric, placement.T, zones.T)


def whole(state, metric, placement, zones):
    flat = state.reshape(4 * L * ROWS, LANES)
    ground = metric.reshape(3 * ROWS, LANES)
    V, A = VMEM_SPEC, ANY_SPEC
    axes = ("nest", "gx", "gy")
    DMA = pltpu.SemaphoreType.DMA

    def pairs_of(axis, step, groups):
        pairs = []
        for n in groups:
            for x in range(8):
                for y in range(8):
                    to = (x + step, y) if axis == 0 else (x, y + step)
                    if 0 <= to[axis] < 8:
                        pairs.append(((n * 8 + x) * 8 + y, (n * 8 + to[0]) * 8 + to[1]))
        return pairs

    def shifted(value, axis, step, groups):
        return lax.ppermute(value, axes, pairs_of(axis, step, groups))

    def rows_halo(flat, ground, groups):
        to_up, to_down = call(edge_kernel, (V, V), [(PLANES * 8, LANES)] * 2)(flat, ground)
        return shifted(to_down, 0, 1, groups), shifted(to_up, 0, -1, groups)

    def packed(flat, ground, from_up, from_down):
        return call(pack_kernel, (V,) * 4, [(96, LANES)] * 2)(flat, ground, from_up, from_down)

    def as_parent(flat, ground, placement):
        mine = (NESTS,)
        slots, info = call(
            select_kernel,
            (A, A),
            [(8, SLOT, LANES), (8, LANES)],
            [
                pltpu.VMEM((3 * L * ROWS, LANES), F32),
                pltpu.VMEM((8, SLOT, LANES), F32),
                pltpu.SMEM((2, NESTS), jnp.int32),
                DMA((4,)),
                DMA((2,)),
            ],
            near=(False, True),
        )(flat, pltpu.with_memory_space_constraint(placement, pltpu.HBM))
        first = lax.all_to_all(slots, "gy", 0, 0).reshape(8 * SLOT, LANES)
        from_up, from_down = rows_halo(flat, ground, mine)
        (second,) = call(
            spread_kernel,
            (V, V),
            [(8 * FINE, LANES)],
            [pltpu.VMEM((8 * FINE, LANES), F32), DMA((2,))],
            near=False,
        )(first, info)
        arrived = lax.all_to_all(second.reshape(8, FINE, LANES), "gx", 0, 0).reshape(8 * FINE, LANES)
        left, right = packed(flat, ground, from_up, from_down)
        parts = call(merge_kernel, (V, V), [(THREE, LANES), (THREE, LANES), (8, LANES)])(arrived, info)
        return (from_up, from_down, left, right, *parts)

    def as_nest(flat, ground, placement):
        others = range(NESTS)
        from_up, from_down = rows_halo(flat, ground, others)
        left, right = packed(flat, ground, from_up, from_down)
        none = jnp.zeros((THREE, LANES), F32)
        return from_up, from_down, left, right, none, none, none[:8]

    from_up, from_down, left, right, across, beyond, along = lax.cond(
        lax.axis_index("nest") == NESTS, as_parent, as_nest, flat, ground, placement
    )

    def send(value, place):
        pairs = []
        for n in range(NESTS):
            for g in range(8):
                x, y = place(g, PIECE[n][g])
                pairs.append(((NESTS * 8 + g) * 8 + SEAT[n], (n * 8 + x) * 8 + y))
        return lax.ppermute(value, axes, pairs)

    west = send(across, lambda g, q: (0, q))
    east = send(beyond, lambda g, q: (7, q))
    top = send(along, lambda g, q: (g, 7))
    bottom = send(along, lambda g, q: (g, 0))
    everyone = range(NESTS + 1)
    from_left, from_right = shifted(right, 1, 1, everyone), shifted(left, 1, -1, everyone)
    flat, ground, from_up, from_down = call(
        fetch_kernel,
        (A,) * 4,
        [(4 * L * ROWS, LANES), (3 * ROWS, LANES), (PLANES * 8, LANES), (PLANES * 8, LANES)],
        [DMA((4,))],
    )(flat, ground, from_up, from_down)
    (moved,) = call(
        advance_kernel,
        (V,) * 6,
        [(4 * L * ROWS, LANES)],
        [pltpu.VMEM((4 * L, 2, EXT, LANES), F32), pltpu.VMEM((4, 2, EXT, LANES), F32)],
    )(flat, ground, from_up, from_down, from_left, from_right)
    (result,) = call(
        relax_kernel,
        (V,) * 6,
        [(4 * L * ROWS, LANES)],
        [pltpu.VMEM((4 * L * ROWS, LANES), F32), DMA((4,))],
        near=False,
    )(moved, west, east, bottom, top, zones)
    return result.reshape(state.shape)


def solution(mesh):
    return jax.shard_map(
        local,
        mesh=mesh,
        in_specs=(P("nest", None, None, "gx", "gy"), P("nest", None, "gx", "gy"), P(), P()),
        out_specs=P("nest", None, None, "gx", "gy"),
        check_vma=False,
    )
```

```python
import jax
import jax.numpy as jnp
from jax import lax
from jax.experimental import pallas as pl
from jax.experimental.pallas import tpu as pltpu
from jax.sharding import PartitionSpec as P


SUB = 4
R = 3
W_MAX = 5
L = 8
NESTS = 7
HALO = 8
ROWS = 16
LANES = 128
PLANES = 4 * L + 3
SLOT = 64
FINE = 32
X_ROWS = 48
THREE = 24
N_X = 128
N_Y = 1024
EAST = (N_X - 1) // R - 1
NORTH = (N_Y - 1) // R - 2
F32 = jnp.float32
HIGH = lax.Precision.HIGHEST

SEAT = (4, 1, 7, 2, 6, 3, 5)

SEAT = (7, 1, 5, 2, 3, 6, 4)
SPARE = 0


def ring(a, b):
    return min((a - b) % 8, (b - a) % 8)


def pieces_of(n):
    far = sorted(range(8), key=lambda q: -ring(4 + SEAT[n] // 2, 4 * (n % 2) + q // 2))
    near = sorted(range(8), key=lambda g: max(ring(g, 0), ring(g, 7)))
    return tuple(q for _, q in sorted(zip(near, far)))


PIECE = tuple(pieces_of(n) for n in range(NESTS))

VMEM_SPEC = pl.BlockSpec(memory_space=pltpu.VMEM)


def iota(shape, dim):
    return lax.broadcasted_iota(jnp.int32, shape, dim)


def plane_row(state, metric, plane, row, count):
    if plane < 4 * L:
        return state[plane * ROWS + row : plane * ROWS + row + count, :]
    start = (plane - 4 * L) * ROWS + row
    return metric[start : start + count, :]


def select_kernel(state, where, slots, info, fields, store, placement, sems, out_sems):
    gx = lax.axis_index("gx")
    gy = lax.axis_index("gy")
    ask = pltpu.make_async_copy(where, placement, sems.at[3])
    ask.start()
    loads = []
    for t, field in enumerate((0, 1, 3)):
        rows = pl.ds(field * L * ROWS, L * ROWS)
        loads.append(pltpu.make_async_copy(state.at[rows], fields.at[pl.ds(t * L * ROWS, L * ROWS)], sems.at[t]))
        loads[-1].start()
    ask.wait()
    rows_n = iota((THREE, LANES), 0)
    first = jnp.zeros((THREE, LANES), jnp.int32)
    bases = []
    for n in range(NESTS):
        low = placement[0, n] - ROWS * gx
        bases.append(jnp.where((low >= -1) & (low < ROWS), low, low + EAST))
        low = placement[1, n] - LANES * gy
        base = jnp.where((low >= -1) & (low < LANES), low, low + NORTH)
        first = jnp.where((rows_n >= 3 * n) & (rows_n < 3 * n + 3), base + rows_n - 3 * n, first)
    pick = (iota((THREE, LANES), 1) == first).astype(F32)
    store[SPARE] = jnp.zeros((SLOT, LANES), F32)
    for t in range(3):
        loads[t].wait()
        start = t * L * ROWS
        for n in range(NESTS):
            for a in range(2):
                row = jnp.clip(bases[n] + a, 0, ROWS - 1)
                out = a * THREE + t * L
                store[SEAT[n], out : out + L, :] = fields[pl.ds(start + row, L, stride=ROWS), :]
    lower = pltpu.make_async_copy(store.at[:, 0:X_ROWS], slots.at[:, 0:X_ROWS], out_sems.at[0])
    lower.start()
    line, spot = iota((8, LANES), 0), iota((8, LANES), 1)
    kept = jnp.zeros((8, LANES), F32)
    for n in range(NESTS):
        pair = jnp.where(line == 0, placement[0, n], placement[1, n]).astype(F32)
        kept = jnp.where(spot == n, pair, kept)
    info[...] = kept
    for t in range(3):
        start = t * L * ROWS
        cols = lax.dot_general(
            pick, fields[start : start + 128, :], (((1,), (1,)), ((), ())), precision=HIGH, preferred_element_type=F32
        )
        for n in range(NESTS):
            store[SEAT[n], X_ROWS + 3 * t : X_ROWS + 3 * t + 3, :] = cols[3 * n : 3 * n + 3, :]
    for n in range(NESTS):
        store[SEAT[n], X_ROWS + 9 : SLOT, :] = jnp.zeros((7, LANES), F32)
    upper = pltpu.make_async_copy(store.at[:, X_ROWS:SLOT], slots.at[:, X_ROWS:SLOT], out_sems.at[1])
    upper.start()
    lower.wait()
    upper.wait()


def edge_kernel(state, metric, up, down):
    for plane in range(PLANES):
        up[plane * 8 : plane * 8 + 8, :] = plane_row(state, metric, plane, 0, 8)
        down[plane * 8 : plane * 8 + 8, :] = plane_row(state, metric, plane, 8, 8)


def fetch_kernel(state, metric, fields, ground, sems):
    copies = [pltpu.make_async_copy(a, b, sems.at[i]) for i, (a, b) in enumerate(((state, fields), (metric, ground)))]
    for one in copies:
        one.start()
    for one in copies:
        one.wait()


def strip(state, metric, from_up, from_down, plane, rt):
    if rt == 0:
        return from_up[plane * 8 : plane * 8 + 8, :]
    if rt == 3:
        return from_down[plane * 8 : plane * 8 + 8, :]
    return plane_row(state, metric, plane, (rt - 1) * 8, 8)


def pack_kernel(state, metric, from_up, from_down, left, right, above, below):
    above[...] = from_up[...]
    below[...] = from_down[...]
    lane = iota((8, LANES), 1) // 8
    for rt in range(4):
        for group in range(3):
            left_sum = jnp.zeros((8, LANES), F32)
            right_sum = jnp.zeros((8, LANES), F32)
            for s in range(16):
                plane = group * 16 + s
                if plane >= PLANES:
                    break
                value = strip(state, metric, from_up, from_down, plane, rt)
                left_sum = jnp.where(lane == s, pltpu.roll(value, 8 * s, 1) if s else value, left_sum)
                shift = (8 * s + 8) % LANES
                right_sum = jnp.where(lane == s, pltpu.roll(value, shift, 1) if shift else value, right_sum)
            at = (rt * 3 + group) * 8
            left[at : at + 8, :] = left_sum
            right[at : at + 8, :] = right_sum


def next_col(centre, halo, lane):
    edge = lane == 0
    return (
        pltpu.roll(jnp.where(edge, halo, centre), LANES - 1, 1),
        pltpu.roll(jnp.where(edge, centre, halo), LANES - 1, 1),
    )


def prev_col(centre, halo, lane):
    edge = lane == LANES - 1
    return pltpu.roll(jnp.where(edge, halo, centre), 1, 1), pltpu.roll(jnp.where(edge, centre, halo), 1, 1)


EXT = ROWS + 2 * HALO


def advance_kernel(state, metric, from_up, from_down, from_left, from_right, out, wide, terrain):
    gx = lax.axis_index("gx")
    gy = lax.axis_index("gy")
    lane8 = iota((8, LANES), 1)
    for plane in range(PLANES):
        group, s = divmod(plane, 16)
        for rt in range(4):
            at = (rt * 3 + group) * 8
            right_part = pltpu.roll(from_right[at : at + 8, :], (LANES - 8 * s) % LANES, 1)
            left_part = pltpu.roll(from_left[at : at + 8, :], (120 - 8 * s) % LANES, 1)
            halo = jnp.where(lane8 < 8, right_part, jnp.where(lane8 >= 120, left_part, 0.0))
            centre = strip(state, metric, from_up, from_down, plane, rt)
            if plane < 4 * L:
                wide[plane, 0, rt * 8 : rt * 8 + 8, :] = centre
                wide[plane, 1, rt * 8 : rt * 8 + 8, :] = halo
            else:
                terrain[plane - 4 * L, 0, rt * 8 : rt * 8 + 8, :] = centre
                terrain[plane - 4 * L, 1, rt * 8 : rt * 8 + 8, :] = halo

    row = iota((EXT, LANES), 0) + ROWS * gx - HALO
    lane = iota((EXT, LANES), 1)
    row_in = (row >= 0) & (row < N_X)
    last = lax.axis_size("gy") - 1
    halo_in = row_in & (((lane < 8) & (gy < last)) | ((lane >= 120) & (gy > 0)))
    for tile, inside in ((0, row_in), (1, halo_in)):
        inverse = 1.0 / jnp.where(inside, terrain[2, tile], 1.0)
        terrain[2, tile] = inverse
        terrain[3, tile] = jnp.where(inside, 0.5, 0.0)

    def substep(_, carry):
        for k in range(L):
            up, low = min(k + 1, L - 1), max(k - 1, 0)
            sigma = 1.0 - (k + 0.5) / L
            centre, halo = wide[24 + k, 0], wide[24 + k, 1]
            east = next_col(centre, halo, lane)
            west = prev_col(centre, halo, lane)
            for tile in range(2):
                here = (centre, halo)[tile]
                step = terrain[3, tile]
                press_z = (wide[24 + up, tile] - wide[24 + low, tile]) * (0.5 * terrain[2, tile])
                grad_x = (pltpu.roll(here, EXT - 1, 0) - pltpu.roll(here, 1, 0)) * 0.5
                grad_y = (east[tile] - west[tile]) * 0.5
                lean = sigma * press_z
                wide[k, tile] = wide[k, tile] - step * (grad_x - terrain[0, tile] * lean)
                wide[8 + k, tile] = wide[8 + k, tile] - step * (grad_y - terrain[1, tile] * lean)
                wide[16 + k, tile] = wide[16 + k, tile] - 0.5 * press_z
        for k in range(L):
            up, low = min(k + 1, L - 1), max(k - 1, 0)
            sigma = 1.0 - (k + 0.5) / L
            north = next_col(wide[8 + k, 0], wide[8 + k, 1], lane)
            south = prev_col(wide[8 + k, 0], wide[8 + k, 1], lane)
            for tile in range(2):
                wind = wide[k, tile]
                flat = pltpu.roll(wind, EXT - 1, 0) - pltpu.roll(wind, 1, 0) + north[tile] - south[tile]
                slope = terrain[0, tile] * (wide[up, tile] - wide[low, tile])
                slope = slope + terrain[1, tile] * (wide[8 + up, tile] - wide[8 + low, tile])
                rise = wide[16 + up, tile] - wide[16 + low, tile]
                spread = 0.5 * (flat + terrain[2, tile] * (rise - sigma * slope))
                wide[24 + k, tile] = wide[24 + k, tile] - terrain[3, tile] * spread
        return carry

    lax.fori_loop(0, SUB, substep, 0)
    for plane in range(4 * L):
        out[plane * ROWS : plane * ROWS + ROWS, :] = wide[plane, 0, HALO : HALO + ROWS, :]


def seated(seat):
    nest = 0
    for n in range(1, NESTS):
        nest = jnp.where(seat == SEAT[n], n, nest)
    return nest


def corner(placement, nest):
    both = placement[...]
    mine = iota(both.shape, 1) == nest
    one = [jnp.sum(jnp.where(mine & (iota(both.shape, 0) == d), both, 0.0)) for d in range(2)]
    return one[0].astype(jnp.int32), one[1].astype(jnp.int32)


def spread_kernel(got, placement, slots, store, sems):
    gx = lax.axis_index("gx")
    nest = seated(lax.axis_index("gy"))
    ox, oy = corner(placement, nest)
    lane = iota((THREE, LANES), 1)

    def line(col, b, c):
        return got[pl.ds((col // LANES) * SLOT + X_ROWS + 3 * c + b, 1), :]

    south = [[line(oy + b, b, c) for c in range(3)] for b in range(2)]
    north = [[line(oy + NORTH + b, b, c) for c in range(3)] for b in range(3)]
    even = jnp.concatenate(south[0] + north[0] + [north[2][0], north[2][2]], 0)
    odd = jnp.concatenate(south[1] + north[1] + [north[2][1], north[2][2]], 0)
    half = iota((8, LANES), 1) % ROWS < 8
    copies = [
        pltpu.make_async_copy(store.at[pl.ds(h * 4 * FINE, 4 * FINE)], slots.at[pl.ds(h * 4 * FINE, 4 * FINE)], sems.at[h])
        for h in range(2)
    ]
    for g in range(8):
        reach = 0
        for n in range(NESTS):
            reach = jnp.where(nest == n, (LANES * PIECE[n][g]) // R, reach)
        start = oy + reach
        low = start // LANES
        high = jnp.minimum(low + 1, 7)
        shift = start % LANES
        parts = []
        for a in range(2):
            near = got[pl.ds(pl.multiple_of(low * SLOT + a * THREE, 8), THREE), :]
            far = got[pl.ds(pl.multiple_of(high * SLOT + a * THREE, 8), THREE), :]
            parts.append(pltpu.roll(jnp.where(lane >= shift, near, far), (LANES + 64 * a - shift) % LANES, 1))
        store[g * FINE : g * FINE + THREE, :] = jnp.where(lane < 64, parts[0], parts[1])
        turn = ROWS * gx - ox - (ROWS * g) // R + 4 * LANES
        store[g * FINE + THREE : g * FINE + FINE, :] = jnp.where(
            half, pltpu.roll(even, turn % LANES, 1), pltpu.roll(odd, (turn + 8) % LANES, 1)
        )
        if g % 4 == 3:
            copies[g // 4].start()
    for h in range(2):
        copies[h].wait()


def merge_kernel(got, placement, west, east, along):
    nest = seated(lax.axis_index("gy"))
    ox, _ = corner(placement, nest)
    lane = iota((THREE, LANES), 1)

    def rows(row):
        return got[pl.ds(pl.multiple_of((row // ROWS) * FINE, 8), THREE), :]

    west[...] = jnp.where(lane < 64, rows(ox), rows(ox + 1))
    east[...] = jnp.where(lane < 64, rows(ox + EAST), rows(ox + EAST + 1))
    start = ox + (ROWS * lax.axis_index("gx")) // R
    low = start // ROWS
    high = jnp.minimum(low + 1, 7)
    near = got[pl.ds(pl.multiple_of(low * FINE + THREE, 8), 8), :]
    far = got[pl.ds(pl.multiple_of(high * FINE + THREE, 8), 8), :]
    along[...] = jnp.where(iota((8, LANES), 1) % 8 < ROWS * (low + 1) - start, near, far)


def third(value):
    return (value * 171) >> 9


def relax_kernel(moved, west, east, south, north, zones, out, store, sems):
    group = lax.axis_index("nest")
    gx = lax.axis_index("gx")
    gy = lax.axis_index("gy")
    nest = jnp.minimum(group, NESTS - 1)
    last_x = lax.axis_size("gx") - 1
    size = L * ROWS
    copies = [
        pltpu.make_async_copy((moved if f == 2 else store).at[pl.ds(f * size, size)], out.at[pl.ds(f * size, size)], sems.at[f])
        for f in range(4)
    ]

    @pl.when(group == NESTS)
    def _():
        plain = pltpu.make_async_copy(moved, out, sems.at[0])
        plain.start()
        plain.wait()

    @pl.when(group < NESTS)
    def _():
        copies[2].start()
        source = jnp.where(gx == 0, west[...], east[...])
        index = third(iota((THREE, LANES), 1) + (LANES * gy) % R)
        lines = [jnp.take_along_axis(source, index + 64 * a, axis=1) for a in range(2)]

        big_row, big_lane = iota((LANES, LANES), 0), iota((LANES, LANES), 1)
        need = third(big_row % ROWS + (ROWS * gx) % R)
        pick = ((big_row // ROWS == big_lane // ROWS) & (big_lane % 8 == need)).astype(F32)

        row, col = iota((ROWS, LANES), 0), iota((ROWS, LANES), 1)
        row_pos, col_pos = (row + ROWS * gx).astype(F32), (col + LANES * gy).astype(F32)
        own = jnp.where(iota((4, NESTS), 1) == nest, zones[...].astype(F32), 0.0)
        widths = jnp.sum(own, axis=1, keepdims=True)
        weight = jnp.zeros((ROWS, LANES), F32)
        for edge, dist in enumerate((row_pos, N_X - 1 - row_pos, col_pos, N_Y - 1 - col_pos)):
            width = jnp.broadcast_to(widths[edge : edge + 1, :], (ROWS, LANES))
            weight = jnp.maximum(weight, jnp.maximum((width - dist) / width, 0.0))
        weight = jnp.where(group < NESTS, weight, 0.0)
        in_x = ((gx == 0) & (row < W_MAX)) | ((gx == last_x) & (row >= ROWS - W_MAX))
        split = jnp.where(gx == 0, 3, ROWS - 2)

        lane8, row8 = iota((8, LANES), 1), iota((8, LANES), 0)
        first_half = lane8 % ROWS < 8
        for c, field in enumerate((0, 1, 3)):
            pair = jnp.broadcast_to(south[c : c + 1, :], (8, LANES))
            low = jnp.where(first_half == (row8 < 3), pair, 0.0)
            low = jnp.where(row8 < W_MAX, low, 0.0)
            pair = jnp.broadcast_to(north[3 + c : 4 + c, :], (8, LANES))
            last = jnp.broadcast_to(north[(6, 6, 7)[c] : (7, 7, 8)[c], :], (8, LANES))
            last = jnp.where(first_half == (c != 1), last, 0.0)
            high = jnp.where(first_half == (row8 < 4), pair, 0.0)
            high = jnp.where(row8 == 7, last, jnp.where(row8 >= 3, high, 0.0))
            table = jnp.concatenate([low, jnp.zeros((112, LANES), F32), high], 0)
            along = lax.dot_general(pick, table, (((1,), (1,)), ((), ())), precision=HIGH, preferred_element_type=F32)
            for k in range(L):
                plane = c * L + k
                line0 = jnp.broadcast_to(lines[0][plane : plane + 1, :], (ROWS, LANES))
                line1 = jnp.broadcast_to(lines[1][plane : plane + 1, :], (ROWS, LANES))
                target = jnp.where(in_x, jnp.where(row < split, line0, line1), along[k * ROWS : k * ROWS + ROWS, :])
                at = (field * L + k) * ROWS
                value = moved[at : at + ROWS, :]
                store[at : at + ROWS, :] = value + weight * (target - value)
            copies[field].start()
        for f in range(4):
            copies[f].wait()


ANY_SPEC = pl.BlockSpec(memory_space=pl.ANY)


def call(kernel, specs, outs, scratch=(), near=True):
    places = near if isinstance(near, tuple) else (near,) * len(outs)
    many = tuple(pltpu.VMEM(shape, F32) if near_by else jax.ShapeDtypeStruct(shape, F32) for shape, near_by in zip(outs, places))
    run = pl.pallas_call(
        kernel,
        in_specs=list(specs),
        out_specs=tuple(VMEM_SPEC if near_by else ANY_SPEC for near_by in places),
        out_shape=many,
        scratch_shapes=list(scratch),
    )

    def placed(*args):
        return run(*(a if s is ANY_SPEC else pltpu.with_memory_space_constraint(a, s.memory_space) for a, s in zip(args, specs)))

    return placed


def local(state, metric, placement, zones):
    return whole(state, metric, placement.T, zones.T)


def whole(state, metric, placement, zones):
    flat = state.reshape(4 * L * ROWS, LANES)
    ground = metric.reshape(3 * ROWS, LANES)
    V, A = VMEM_SPEC, ANY_SPEC
    axes = ("nest", "gx", "gy")
    DMA = pltpu.SemaphoreType.DMA

    def pairs_of(axis, step, groups):
        pairs = []
        for n in groups:
            for x in range(8):
                for y in range(8):
                    to = (x + step, y) if axis == 0 else (x, y + step)
                    if 0 <= to[axis] < 8:
                        pairs.append(((n * 8 + x) * 8 + y, (n * 8 + to[0]) * 8 + to[1]))
        return pairs

    def shifted(value, axis, step, groups):
        return lax.ppermute(value, axes, pairs_of(axis, step, groups))

    def rows_halo(flat, ground, groups):
        to_up, to_down = call(edge_kernel, (V, V), [(PLANES * 8, LANES)] * 2)(flat, ground)
        return shifted(to_down, 0, 1, groups), shifted(to_up, 0, -1, groups)

    def packed(flat, ground, from_up, from_down):
        return call(pack_kernel, (V,) * 4, [(96, LANES)] * 2 + [(PLANES * 8, LANES)] * 2)(
            flat, ground, from_up, from_down
        )

    def as_parent(flat, ground, placement):
        mine = (NESTS,)
        slots, info = call(
            select_kernel,
            (A, A),
            [(8, SLOT, LANES), (8, LANES)],
            [
                pltpu.VMEM((3 * L * ROWS, LANES), F32),
                pltpu.VMEM((8, SLOT, LANES), F32),
                pltpu.SMEM((2, NESTS), jnp.int32),
                DMA((4,)),
                DMA((2,)),
            ],
            near=(False, True),
        )(flat, pltpu.with_memory_space_constraint(placement, pltpu.HBM))
        first = lax.all_to_all(slots, "gy", 0, 0).reshape(8 * SLOT, LANES)
        from_up, from_down = rows_halo(flat, ground, mine)
        (second,) = call(
            spread_kernel,
            (V, V),
            [(8 * FINE, LANES)],
            [pltpu.VMEM((8 * FINE, LANES), F32), DMA((2,))],
            near=False,
        )(first, info)
        arrived = lax.all_to_all(second.reshape(8, FINE, LANES), "gx", 0, 0).reshape(8 * FINE, LANES)
        left, right, above, below = packed(flat, ground, from_up, from_down)
        parts = call(merge_kernel, (V, V), [(THREE, LANES), (THREE, LANES), (8, LANES)])(arrived, info)
        return (above, below, left, right, *parts)

    def as_nest(flat, ground, placement):
        others = range(NESTS)
        from_up, from_down = rows_halo(flat, ground, others)
        left, right, above, below = packed(flat, ground, from_up, from_down)
        none = jnp.zeros((THREE, LANES), F32)
        return above, below, left, right, none, none, none[:8]

    from_up, from_down, left, right, across, beyond, along = lax.cond(
        lax.axis_index("nest") == NESTS, as_parent, as_nest, flat, ground, placement
    )

    def send(value, place):
        pairs = []
        for n in range(NESTS):
            for g in range(8):
                x, y = place(g, PIECE[n][g])
                pairs.append(((NESTS * 8 + g) * 8 + SEAT[n], (n * 8 + x) * 8 + y))
        return lax.ppermute(value, axes, pairs)

    west = send(across, lambda g, q: (0, q))
    east = send(beyond, lambda g, q: (7, q))
    top = send(along, lambda g, q: (g, 7))
    bottom = send(along, lambda g, q: (g, 0))
    everyone = range(NESTS + 1)
    from_left, from_right = shifted(right, 1, 1, everyone), shifted(left, 1, -1, everyone)
    flat, ground = call(fetch_kernel, (A, A), [(4 * L * ROWS, LANES), (3 * ROWS, LANES)], [DMA((2,))])(flat, ground)
    (moved,) = call(
        advance_kernel,
        (V,) * 6,
        [(4 * L * ROWS, LANES)],
        [pltpu.VMEM((4 * L, 2, EXT, LANES), F32), pltpu.VMEM((4, 2, EXT, LANES), F32)],
    )(flat, ground, from_up, from_down, from_left, from_right)
    (result,) = call(
        relax_kernel,
        (V,) * 6,
        [(4 * L * ROWS, LANES)],
        [pltpu.VMEM((4 * L * ROWS, LANES), F32), DMA((4,))],
        near=False,
    )(moved, west, east, bottom, top, zones)
    return result.reshape(state.shape)


def solution(mesh):
    return jax.shard_map(
        local,
        mesh=mesh,
        in_specs=(P("nest", None, None, "gx", "gy"), P("nest", None, "gx", "gy"), P(), P()),
        out_specs=P("nest", None, None, "gx", "gy"),
        check_vma=False,
    )
```

```python
import jax
import jax.numpy as jnp
from jax import lax
from jax.experimental import pallas as pl
from jax.experimental.pallas import tpu as pltpu
from jax.sharding import PartitionSpec as P


SUB = 4
R = 3
W_MAX = 5
L = 8
NESTS = 7
HALO = 8
ROWS = 16
LANES = 128
PLANES = 4 * L + 3
SLOT = 64
FINE = 32
X_ROWS = 48
THREE = 24
N_X = 128
N_Y = 1024
EAST = (N_X - 1) // R - 1
NORTH = (N_Y - 1) // R - 2
F32 = jnp.float32
HIGH = lax.Precision.HIGHEST

SEAT = (4, 1, 7, 2, 6, 3, 5)

SEAT = (7, 1, 5, 2, 3, 6, 4)
SPARE = 0


def ring(a, b):
    return min((a - b) % 8, (b - a) % 8)


def pieces_of(n):
    far = sorted(range(8), key=lambda q: -ring(4 + SEAT[n] // 2, 4 * (n % 2) + q // 2))
    near = sorted(range(8), key=lambda g: max(ring(g, 0), ring(g, 7)))
    return tuple(q for _, q in sorted(zip(near, far)))


PIECE = tuple(pieces_of(n) for n in range(NESTS))

VMEM_SPEC = pl.BlockSpec(memory_space=pltpu.VMEM)


def iota(shape, dim):
    return lax.broadcasted_iota(jnp.int32, shape, dim)


def plane_row(state, metric, plane, row, count):
    if plane < 4 * L:
        return state[plane * ROWS + row : plane * ROWS + row + count, :]
    start = (plane - 4 * L) * ROWS + row
    return metric[start : start + count, :]


def select_kernel(state, where, slots, info, fields, store, placement, sems, out_sems):
    gx = lax.axis_index("gx")
    gy = lax.axis_index("gy")
    ask = pltpu.make_async_copy(where, placement, sems.at[3])
    ask.start()
    loads = []
    for t, field in enumerate((0, 1, 3)):
        rows = pl.ds(field * L * ROWS, L * ROWS)
        loads.append(pltpu.make_async_copy(state.at[rows], fields.at[pl.ds(t * L * ROWS, L * ROWS)], sems.at[t]))
        loads[-1].start()
    ask.wait()
    rows_n = iota((THREE, LANES), 0)
    first = jnp.zeros((THREE, LANES), jnp.int32)
    bases = []
    for n in range(NESTS):
        low = placement[0, n] - ROWS * gx
        bases.append(jnp.where((low >= -1) & (low < ROWS), low, low + EAST))
        low = placement[1, n] - LANES * gy
        base = jnp.where((low >= -1) & (low < LANES), low, low + NORTH)
        first = jnp.where((rows_n >= 3 * n) & (rows_n < 3 * n + 3), base + rows_n - 3 * n, first)
    pick = (iota((THREE, LANES), 1) == first).astype(F32)
    store[SPARE] = jnp.zeros((SLOT, LANES), F32)
    for t in range(3):
        loads[t].wait()
        start = t * L * ROWS
        for n in range(NESTS):
            for a in range(2):
                row = jnp.clip(bases[n] + a, 0, ROWS - 1)
                out = a * THREE + t * L
                store[SEAT[n], out : out + L, :] = fields[pl.ds(start + row, L, stride=ROWS), :]
    lower = pltpu.make_async_copy(store.at[:, 0:X_ROWS], slots.at[:, 0:X_ROWS], out_sems.at[0])
    lower.start()
    line, spot = iota((8, LANES), 0), iota((8, LANES), 1)
    kept = jnp.zeros((8, LANES), F32)
    for n in range(NESTS):
        pair = jnp.where(line == 0, placement[0, n], placement[1, n]).astype(F32)
        kept = jnp.where(spot == n, pair, kept)
    info[...] = kept
    for t in range(3):
        start = t * L * ROWS
        cols = lax.dot_general(
            pick, fields[start : start + 128, :], (((1,), (1,)), ((), ())), precision=HIGH, preferred_element_type=F32
        )
        for n in range(NESTS):
            store[SEAT[n], X_ROWS + 3 * t : X_ROWS + 3 * t + 3, :] = cols[3 * n : 3 * n + 3, :]
    for n in range(NESTS):
        store[SEAT[n], X_ROWS + 9 : SLOT, :] = jnp.zeros((7, LANES), F32)
    upper = pltpu.make_async_copy(store.at[:, X_ROWS:SLOT], slots.at[:, X_ROWS:SLOT], out_sems.at[1])
    upper.start()
    lower.wait()
    upper.wait()


def edge_kernel(state, metric, up, down):
    for plane in range(PLANES):
        up[plane * 8 : plane * 8 + 8, :] = plane_row(state, metric, plane, 0, 8)
        down[plane * 8 : plane * 8 + 8, :] = plane_row(state, metric, plane, 8, 8)


def fetch_kernel(state, metric, fields, ground, sems):
    copies = [pltpu.make_async_copy(a, b, sems.at[i]) for i, (a, b) in enumerate(((state, fields), (metric, ground)))]
    for one in copies:
        one.start()
    for one in copies:
        one.wait()


def strip(state, metric, from_up, from_down, plane, rt):
    if rt == 0:
        return from_up[plane * 8 : plane * 8 + 8, :]
    if rt == 3:
        return from_down[plane * 8 : plane * 8 + 8, :]
    return plane_row(state, metric, plane, (rt - 1) * 8, 8)


def pack_kernel(state, metric, from_up, from_down, far, near, above, below):
    odd = lax.axis_index("gy") % 2 == 1
    above[...] = from_up[...]
    below[...] = from_down[...]
    lane = iota((8, LANES), 1) // 8
    for rt in range(4):
        for group in range(3):
            left_sum = jnp.zeros((8, LANES), F32)
            right_sum = jnp.zeros((8, LANES), F32)
            for s in range(16):
                plane = group * 16 + s
                if plane >= PLANES:
                    break
                value = strip(state, metric, from_up, from_down, plane, rt)
                left_sum = jnp.where(lane == s, pltpu.roll(value, 8 * s, 1) if s else value, left_sum)
                shift = (8 * s + 8) % LANES
                right_sum = jnp.where(lane == s, pltpu.roll(value, shift, 1) if shift else value, right_sum)
            at = (rt * 3 + group) * 8
            far[at : at + 8, :] = jnp.where(odd, right_sum, left_sum)
            near[at : at + 8, :] = jnp.where(odd, left_sum, right_sum)


def next_col(centre, halo, lane):
    edge = lane == 0
    return (
        pltpu.roll(jnp.where(edge, halo, centre), LANES - 1, 1),
        pltpu.roll(jnp.where(edge, centre, halo), LANES - 1, 1),
    )


def prev_col(centre, halo, lane):
    edge = lane == LANES - 1
    return pltpu.roll(jnp.where(edge, halo, centre), 1, 1), pltpu.roll(jnp.where(edge, centre, halo), 1, 1)


EXT = ROWS + 2 * HALO


def advance_kernel(state, metric, from_up, from_down, from_far, from_near, out, wide, terrain):
    gx = lax.axis_index("gx")
    gy = lax.axis_index("gy")
    odd = gy % 2 == 1
    lane8 = iota((8, LANES), 1)
    for rt in range(4):
        for group in range(3):
            at = (rt * 3 + group) * 8
            far, near = from_far[at : at + 8, :], from_near[at : at + 8, :]
            from_left, from_right = jnp.where(odd, near, far), jnp.where(odd, far, near)
            for s in range(min(16, PLANES - group * 16)):
                plane = group * 16 + s
                right_part = pltpu.roll(from_right, (LANES - 8 * s) % LANES, 1)
                left_part = pltpu.roll(from_left, (120 - 8 * s) % LANES, 1)
                halo = jnp.where(lane8 < 8, right_part, jnp.where(lane8 >= 120, left_part, 0.0))
                centre = strip(state, metric, from_up, from_down, plane, rt)
                if plane < 4 * L:
                    wide[plane, 0, rt * 8 : rt * 8 + 8, :] = centre
                    wide[plane, 1, rt * 8 : rt * 8 + 8, :] = halo
                else:
                    terrain[plane - 4 * L, 0, rt * 8 : rt * 8 + 8, :] = centre
                    terrain[plane - 4 * L, 1, rt * 8 : rt * 8 + 8, :] = halo

    row = iota((EXT, LANES), 0) + ROWS * gx - HALO
    lane = iota((EXT, LANES), 1)
    row_in = (row >= 0) & (row < N_X)
    last = lax.axis_size("gy") - 1
    halo_in = row_in & (((lane < 8) & (gy < last)) | ((lane >= 120) & (gy > 0)))
    for tile, inside in ((0, row_in), (1, halo_in)):
        inverse = 1.0 / jnp.where(inside, terrain[2, tile], 1.0)
        terrain[2, tile] = inverse
        terrain[3, tile] = jnp.where(inside, 0.5, 0.0)

    def substep(_, carry):
        for k in range(L):
            up, low = min(k + 1, L - 1), max(k - 1, 0)
            sigma = 1.0 - (k + 0.5) / L
            centre, halo = wide[24 + k, 0], wide[24 + k, 1]
            east = next_col(centre, halo, lane)
            west = prev_col(centre, halo, lane)
            for tile in range(2):
                here = (centre, halo)[tile]
                step = terrain[3, tile]
                press_z = (wide[24 + up, tile] - wide[24 + low, tile]) * (0.5 * terrain[2, tile])
                grad_x = (pltpu.roll(here, EXT - 1, 0) - pltpu.roll(here, 1, 0)) * 0.5
                grad_y = (east[tile] - west[tile]) * 0.5
                lean = sigma * press_z
                wide[k, tile] = wide[k, tile] - step * (grad_x - terrain[0, tile] * lean)
                wide[8 + k, tile] = wide[8 + k, tile] - step * (grad_y - terrain[1, tile] * lean)
                wide[16 + k, tile] = wide[16 + k, tile] - 0.5 * press_z
        for k in range(L):
            up, low = min(k + 1, L - 1), max(k - 1, 0)
            sigma = 1.0 - (k + 0.5) / L
            north = next_col(wide[8 + k, 0], wide[8 + k, 1], lane)
            south = prev_col(wide[8 + k, 0], wide[8 + k, 1], lane)
            for tile in range(2):
                wind = wide[k, tile]
                flat = pltpu.roll(wind, EXT - 1, 0) - pltpu.roll(wind, 1, 0) + north[tile] - south[tile]
                slope = terrain[0, tile] * (wide[up, tile] - wide[low, tile])
                slope = slope + terrain[1, tile] * (wide[8 + up, tile] - wide[8 + low, tile])
                rise = wide[16 + up, tile] - wide[16 + low, tile]
                spread = 0.5 * (flat + terrain[2, tile] * (rise - sigma * slope))
                wide[24 + k, tile] = wide[24 + k, tile] - terrain[3, tile] * spread
        return carry

    lax.fori_loop(0, SUB, substep, 0)
    for plane in range(4 * L):
        out[plane * ROWS : plane * ROWS + ROWS, :] = wide[plane, 0, HALO : HALO + ROWS, :]


def seated(seat):
    nest = 0
    for n in range(1, NESTS):
        nest = jnp.where(seat == SEAT[n], n, nest)
    return nest


def corner(placement, nest):
    both = placement[...]
    mine = iota(both.shape, 1) == nest
    one = [jnp.sum(jnp.where(mine & (iota(both.shape, 0) == d), both, 0.0)) for d in range(2)]
    return one[0].astype(jnp.int32), one[1].astype(jnp.int32)


def spread_kernel(got, placement, slots, store, sems):
    gx = lax.axis_index("gx")
    nest = seated(lax.axis_index("gy"))
    ox, oy = corner(placement, nest)
    lane = iota((THREE, LANES), 1)

    def line(col, b, c):
        return got[pl.ds((col // LANES) * SLOT + X_ROWS + 3 * c + b, 1), :]

    south = [[line(oy + b, b, c) for c in range(3)] for b in range(2)]
    north = [[line(oy + NORTH + b, b, c) for c in range(3)] for b in range(3)]
    even = jnp.concatenate(south[0] + north[0] + [north[2][0], north[2][2]], 0)
    odd = jnp.concatenate(south[1] + north[1] + [north[2][1], north[2][2]], 0)
    half = iota((8, LANES), 1) % ROWS < 8
    copies = [
        pltpu.make_async_copy(store.at[pl.ds(h * 4 * FINE, 4 * FINE)], slots.at[pl.ds(h * 4 * FINE, 4 * FINE)], sems.at[h])
        for h in range(2)
    ]
    for g in range(8):
        reach = 0
        for n in range(NESTS):
            reach = jnp.where(nest == n, (LANES * PIECE[n][g]) // R, reach)
        start = oy + reach
        low = start // LANES
        high = jnp.minimum(low + 1, 7)
        shift = start % LANES
        parts = []
        for a in range(2):
            near = got[pl.ds(pl.multiple_of(low * SLOT + a * THREE, 8), THREE), :]
            far = got[pl.ds(pl.multiple_of(high * SLOT + a * THREE, 8), THREE), :]
            parts.append(pltpu.roll(jnp.where(lane >= shift, near, far), (LANES + 64 * a - shift) % LANES, 1))
        store[g * FINE : g * FINE + THREE, :] = jnp.where(lane < 64, parts[0], parts[1])
        turn = ROWS * gx - ox - (ROWS * g) // R + 4 * LANES
        store[g * FINE + THREE : g * FINE + FINE, :] = jnp.where(
            half, pltpu.roll(even, turn % LANES, 1), pltpu.roll(odd, (turn + 8) % LANES, 1)
        )
        if g % 4 == 3:
            copies[g // 4].start()
    for h in range(2):
        copies[h].wait()


def merge_kernel(got, placement, west, east, along):
    nest = seated(lax.axis_index("gy"))
    ox, _ = corner(placement, nest)
    lane = iota((THREE, LANES), 1)

    def rows(row):
        return got[pl.ds(pl.multiple_of((row // ROWS) * FINE, 8), THREE), :]

    west[...] = jnp.where(lane < 64, rows(ox), rows(ox + 1))
    east[...] = jnp.where(lane < 64, rows(ox + EAST), rows(ox + EAST + 1))
    start = ox + (ROWS * lax.axis_index("gx")) // R
    low = start // ROWS
    high = jnp.minimum(low + 1, 7)
    near = got[pl.ds(pl.multiple_of(low * FINE + THREE, 8), 8), :]
    far = got[pl.ds(pl.multiple_of(high * FINE + THREE, 8), 8), :]
    along[...] = jnp.where(iota((8, LANES), 1) % 8 < ROWS * (low + 1) - start, near, far)


def third(value):
    return (value * 171) >> 9


def relax_kernel(moved, west, east, south, north, zones, out, store, sems):
    group = lax.axis_index("nest")
    gx = lax.axis_index("gx")
    gy = lax.axis_index("gy")
    nest = jnp.minimum(group, NESTS - 1)
    last_x = lax.axis_size("gx") - 1
    size = L * ROWS
    copies = [
        pltpu.make_async_copy((moved if f == 2 else store).at[pl.ds(f * size, size)], out.at[pl.ds(f * size, size)], sems.at[f])
        for f in range(4)
    ]

    @pl.when(group == NESTS)
    def _():
        plain = pltpu.make_async_copy(moved, out, sems.at[0])
        plain.start()
        plain.wait()

    @pl.when(group < NESTS)
    def _():
        copies[2].start()
        source = jnp.where(gx == 0, west[...], east[...])
        index = third(iota((THREE, LANES), 1) + (LANES * gy) % R)
        lines = [jnp.take_along_axis(source, index + 64 * a, axis=1) for a in range(2)]

        big_row, big_lane = iota((LANES, LANES), 0), iota((LANES, LANES), 1)
        need = third(big_row % ROWS + (ROWS * gx) % R)
        pick = ((big_row // ROWS == big_lane // ROWS) & (big_lane % 8 == need)).astype(F32)

        row, col = iota((ROWS, LANES), 0), iota((ROWS, LANES), 1)
        row_pos, col_pos = (row + ROWS * gx).astype(F32), (col + LANES * gy).astype(F32)
        own = jnp.where(iota((4, NESTS), 1) == nest, zones[...].astype(F32), 0.0)
        widths = jnp.sum(own, axis=1, keepdims=True)
        weight = jnp.zeros((ROWS, LANES), F32)
        for edge, dist in enumerate((row_pos, N_X - 1 - row_pos, col_pos, N_Y - 1 - col_pos)):
            width = jnp.broadcast_to(widths[edge : edge + 1, :], (ROWS, LANES))
            weight = jnp.maximum(weight, jnp.maximum((width - dist) / width, 0.0))
        weight = jnp.where(group < NESTS, weight, 0.0)
        in_x = ((gx == 0) & (row < W_MAX)) | ((gx == last_x) & (row >= ROWS - W_MAX))
        split = jnp.where(gx == 0, 3, ROWS - 2)

        lane8, row8 = iota((8, LANES), 1), iota((8, LANES), 0)
        first_half = lane8 % ROWS < 8
        for c, field in enumerate((0, 1, 3)):
            pair = jnp.broadcast_to(south[c : c + 1, :], (8, LANES))
            low = jnp.where(first_half == (row8 < 3), pair, 0.0)
            low = jnp.where(row8 < W_MAX, low, 0.0)
            pair = jnp.broadcast_to(north[3 + c : 4 + c, :], (8, LANES))
            last = jnp.broadcast_to(north[(6, 6, 7)[c] : (7, 7, 8)[c], :], (8, LANES))
            last = jnp.where(first_half == (c != 1), last, 0.0)
            high = jnp.where(first_half == (row8 < 4), pair, 0.0)
            high = jnp.where(row8 == 7, last, jnp.where(row8 >= 3, high, 0.0))
            table = jnp.concatenate([low, jnp.zeros((112, LANES), F32), high], 0)
            along = lax.dot_general(pick, table, (((1,), (1,)), ((), ())), precision=HIGH, preferred_element_type=F32)
            for k in range(L):
                plane = c * L + k
                line0 = jnp.broadcast_to(lines[0][plane : plane + 1, :], (ROWS, LANES))
                line1 = jnp.broadcast_to(lines[1][plane : plane + 1, :], (ROWS, LANES))
                target = jnp.where(in_x, jnp.where(row < split, line0, line1), along[k * ROWS : k * ROWS + ROWS, :])
                at = (field * L + k) * ROWS
                value = moved[at : at + ROWS, :]
                store[at : at + ROWS, :] = value + weight * (target - value)
            copies[field].start()
        for f in range(4):
            copies[f].wait()


ANY_SPEC = pl.BlockSpec(memory_space=pl.ANY)


def call(kernel, specs, outs, scratch=(), near=True):
    places = near if isinstance(near, tuple) else (near,) * len(outs)
    many = tuple(pltpu.VMEM(shape, F32) if near_by else jax.ShapeDtypeStruct(shape, F32) for shape, near_by in zip(outs, places))
    run = pl.pallas_call(
        kernel,
        in_specs=list(specs),
        out_specs=tuple(VMEM_SPEC if near_by else ANY_SPEC for near_by in places),
        out_shape=many,
        scratch_shapes=list(scratch),
    )

    def placed(*args):
        return run(*(a if s is ANY_SPEC else pltpu.with_memory_space_constraint(a, s.memory_space) for a, s in zip(args, specs)))

    return placed


def local(state, metric, placement, zones):
    return whole(state, metric, placement.T, zones.T)


def whole(state, metric, placement, zones):
    flat = state.reshape(4 * L * ROWS, LANES)
    ground = metric.reshape(3 * ROWS, LANES)
    V, A = VMEM_SPEC, ANY_SPEC
    axes = ("nest", "gx", "gy")
    DMA = pltpu.SemaphoreType.DMA

    def pairs_of(axis, step, groups):
        pairs = []
        for n in groups:
            for x in range(8):
                for y in range(8):
                    to = (x + step, y) if axis == 0 else (x, y + step)
                    if 0 <= to[axis] < 8:
                        pairs.append(((n * 8 + x) * 8 + y, (n * 8 + to[0]) * 8 + to[1]))
        return pairs

    def shifted(value, axis, step, groups):
        return lax.ppermute(value, axes, pairs_of(axis, step, groups))

    def rows_halo(flat, ground, groups):
        to_up, to_down = call(edge_kernel, (V, V), [(PLANES * 8, LANES)] * 2)(flat, ground)
        return shifted(to_down, 0, 1, groups), shifted(to_up, 0, -1, groups)

    def packed(flat, ground, from_up, from_down):
        return call(pack_kernel, (V,) * 4, [(96, LANES)] * 2 + [(PLANES * 8, LANES)] * 2)(
            flat, ground, from_up, from_down
        )

    def as_parent(flat, ground, placement):
        mine = (NESTS,)
        slots, info = call(
            select_kernel,
            (A, A),
            [(8, SLOT, LANES), (8, LANES)],
            [
                pltpu.VMEM((3 * L * ROWS, LANES), F32),
                pltpu.VMEM((8, SLOT, LANES), F32),
                pltpu.SMEM((2, NESTS), jnp.int32),
                DMA((4,)),
                DMA((2,)),
            ],
            near=(False, True),
        )(flat, pltpu.with_memory_space_constraint(placement, pltpu.HBM))
        first = lax.all_to_all(slots, "gy", 0, 0).reshape(8 * SLOT, LANES)
        from_up, from_down = rows_halo(flat, ground, mine)
        (second,) = call(
            spread_kernel,
            (V, V),
            [(8 * FINE, LANES)],
            [pltpu.VMEM((8 * FINE, LANES), F32), DMA((2,))],
            near=False,
        )(first, info)
        arrived = lax.all_to_all(second.reshape(8, FINE, LANES), "gx", 0, 0).reshape(8 * FINE, LANES)
        far, near, above, below = packed(flat, ground, from_up, from_down)
        parts = call(merge_kernel, (V, V), [(THREE, LANES), (THREE, LANES), (8, LANES)])(arrived, info)
        return (above, below, far, near, *parts)

    def as_nest(flat, ground, placement):
        others = range(NESTS)
        from_up, from_down = rows_halo(flat, ground, others)
        far, near, above, below = packed(flat, ground, from_up, from_down)
        none = jnp.zeros((THREE, LANES), F32)
        return above, below, far, near, none, none, none[:8]

    from_up, from_down, far, near, across, beyond, along = lax.cond(
        lax.axis_index("nest") == NESTS, as_parent, as_nest, flat, ground, placement
    )

    def send(value, place):
        pairs = []
        for n in range(NESTS):
            for g in range(8):
                x, y = place(g, PIECE[n][g])
                pairs.append(((NESTS * 8 + g) * 8 + SEAT[n], (n * 8 + x) * 8 + y))
        return lax.ppermute(value, axes, pairs)

    west = send(across, lambda g, q: (0, q))
    east = send(beyond, lambda g, q: (7, q))
    top = send(along, lambda g, q: (g, 7))
    bottom = send(along, lambda g, q: (g, 0))

    def swapped(value, first):
        pairs = []
        for n in range(NESTS + 1):
            for x in range(8):
                for y in range(first, 7, 2):
                    a = (n * 8 + x) * 8 + y
                    pairs += [(a, a + 1), (a + 1, a)]
        return lax.ppermute(value, axes, pairs)

    from_far = swapped(far, 1)
    from_near = swapped(near, 0)
    flat, ground = call(fetch_kernel, (A, A), [(4 * L * ROWS, LANES), (3 * ROWS, LANES)], [DMA((2,))])(flat, ground)
    (moved,) = call(
        advance_kernel,
        (V,) * 6,
        [(4 * L * ROWS, LANES)],
        [pltpu.VMEM((4 * L, 2, EXT, LANES), F32), pltpu.VMEM((4, 2, EXT, LANES), F32)],
    )(flat, ground, from_up, from_down, from_far, from_near)
    (result,) = call(
        relax_kernel,
        (V,) * 6,
        [(4 * L * ROWS, LANES)],
        [pltpu.VMEM((4 * L * ROWS, LANES), F32), DMA((4,))],
        near=False,
    )(moved, west, east, bottom, top, zones)
    return result.reshape(state.shape)


def solution(mesh):
    return jax.shard_map(
        local,
        mesh=mesh,
        in_specs=(P("nest", None, None, "gx", "gy"), P("nest", None, "gx", "gy"), P(), P()),
        out_specs=P("nest", None, None, "gx", "gy"),
        check_vma=False,
    )
```

```python
import jax
import jax.numpy as jnp
from jax import lax
from jax.experimental import pallas as pl
from jax.experimental.pallas import tpu as pltpu
from jax.sharding import PartitionSpec as P


SUB = 4
R = 3
W_MAX = 5
L = 8
NESTS = 7
HALO = 8
ROWS = 16
LANES = 128
PLANES = 4 * L + 3
SLOT = 64
FINE = 32
X_ROWS = 48
THREE = 24
N_X = 128
N_Y = 1024
EAST = (N_X - 1) // R - 1
NORTH = (N_Y - 1) // R - 2
F32 = jnp.float32
HIGH = lax.Precision.HIGHEST

SEAT = (4, 1, 7, 2, 6, 3, 5)

SEAT = (7, 1, 5, 2, 3, 6, 4)
SPARE = 0


def ring(a, b):
    return min((a - b) % 8, (b - a) % 8)


def pieces_of(n):
    far = sorted(range(8), key=lambda q: -ring(4 + SEAT[n] // 2, 4 * (n % 2) + q // 2))
    near = sorted(range(8), key=lambda g: max(ring(g, 0), ring(g, 7)))
    order = [q for _, q in sorted(zip(near, far))]
    order[3], order[4] = order[4], order[3]
    return tuple(order)


PIECE = tuple(pieces_of(n) for n in range(NESTS))

VMEM_SPEC = pl.BlockSpec(memory_space=pltpu.VMEM)


def iota(shape, dim):
    return lax.broadcasted_iota(jnp.int32, shape, dim)


def plane_row(state, metric, plane, row, count):
    if plane < 4 * L:
        return state[plane * ROWS + row : plane * ROWS + row + count, :]
    start = (plane - 4 * L) * ROWS + row
    return metric[start : start + count, :]


def select_kernel(state, where, slots, info, fields, store, placement, sems, out_sems):
    gx = lax.axis_index("gx")
    gy = lax.axis_index("gy")
    ask = pltpu.make_async_copy(where, placement, sems.at[3])
    ask.start()
    loads = []
    for t, field in enumerate((0, 1, 3)):
        rows = pl.ds(field * L * ROWS, L * ROWS)
        loads.append(pltpu.make_async_copy(state.at[rows], fields.at[pl.ds(t * L * ROWS, L * ROWS)], sems.at[t]))
        loads[-1].start()
    ask.wait()
    rows_n = iota((THREE, LANES), 0)
    first = jnp.zeros((THREE, LANES), jnp.int32)
    bases = []
    for n in range(NESTS):
        low = placement[0, n] - ROWS * gx
        bases.append(jnp.where((low >= -1) & (low < ROWS), low, low + EAST))
        low = placement[1, n] - LANES * gy
        base = jnp.where((low >= -1) & (low < LANES), low, low + NORTH)
        first = jnp.where((rows_n >= 3 * n) & (rows_n < 3 * n + 3), base + rows_n - 3 * n, first)
    pick = (iota((THREE, LANES), 1) == first).astype(F32)
    store[SPARE] = jnp.zeros((SLOT, LANES), F32)
    for t in range(3):
        loads[t].wait()
        start = t * L * ROWS
        for n in range(NESTS):
            for a in range(2):
                row = jnp.clip(bases[n] + a, 0, ROWS - 1)
                out = a * THREE + t * L
                store[SEAT[n], out : out + L, :] = fields[pl.ds(start + row, L, stride=ROWS), :]
    lower = pltpu.make_async_copy(store.at[:, 0:X_ROWS], slots.at[:, 0:X_ROWS], out_sems.at[0])
    lower.start()
    line, spot = iota((8, LANES), 0), iota((8, LANES), 1)
    kept = jnp.zeros((8, LANES), F32)
    for n in range(NESTS):
        pair = jnp.where(line == 0, placement[0, n], placement[1, n]).astype(F32)
        kept = jnp.where(spot == n, pair, kept)
    info[...] = kept
    for t in range(3):
        start = t * L * ROWS
        cols = lax.dot_general(
            pick, fields[start : start + 128, :], (((1,), (1,)), ((), ())), precision=HIGH, preferred_element_type=F32
        )
        for n in range(NESTS):
            store[SEAT[n], X_ROWS + 3 * t : X_ROWS + 3 * t + 3, :] = cols[3 * n : 3 * n + 3, :]
    for n in range(NESTS):
        store[SEAT[n], X_ROWS + 9 : SLOT, :] = jnp.zeros((7, LANES), F32)
    upper = pltpu.make_async_copy(store.at[:, X_ROWS:SLOT], slots.at[:, X_ROWS:SLOT], out_sems.at[1])
    upper.start()
    lower.wait()
    upper.wait()


def edge_kernel(state, metric, up, down):
    for plane in range(PLANES):
        up[plane * 8 : plane * 8 + 8, :] = plane_row(state, metric, plane, 0, 8)
        down[plane * 8 : plane * 8 + 8, :] = plane_row(state, metric, plane, 8, 8)


def strip(state, metric, from_up, from_down, plane, rt):
    if rt == 0:
        return from_up[plane * 8 : plane * 8 + 8, :]
    if rt == 3:
        return from_down[plane * 8 : plane * 8 + 8, :]
    return plane_row(state, metric, plane, (rt - 1) * 8, 8)


def pack_kernel(state, metric, from_up, from_down, far, near, above, below, fields, terrain):
    fields[...] = state[...]
    terrain[...] = metric[...]
    odd = lax.axis_index("gy") % 2 == 1
    above[...] = from_up[...]
    below[...] = from_down[...]
    lane = iota((8, LANES), 1) // 8
    for rt in range(4):
        for group in range(3):
            left_sum = jnp.zeros((8, LANES), F32)
            right_sum = jnp.zeros((8, LANES), F32)
            for s in range(16):
                plane = group * 16 + s
                if plane >= PLANES:
                    break
                value = strip(state, metric, from_up, from_down, plane, rt)
                left_sum = jnp.where(lane == s, pltpu.roll(value, 8 * s, 1) if s else value, left_sum)
                shift = (8 * s + 8) % LANES
                right_sum = jnp.where(lane == s, pltpu.roll(value, shift, 1) if shift else value, right_sum)
            at = (rt * 3 + group) * 8
            far[at : at + 8, :] = jnp.where(odd, right_sum, left_sum)
            near[at : at + 8, :] = jnp.where(odd, left_sum, right_sum)


def next_col(centre, halo, lane):
    edge = lane == 0
    return (
        pltpu.roll(jnp.where(edge, halo, centre), LANES - 1, 1),
        pltpu.roll(jnp.where(edge, centre, halo), LANES - 1, 1),
    )


def prev_col(centre, halo, lane):
    edge = lane == LANES - 1
    return pltpu.roll(jnp.where(edge, halo, centre), 1, 1), pltpu.roll(jnp.where(edge, centre, halo), 1, 1)


EXT = ROWS + 2 * HALO


def advance_kernel(state, metric, from_up, from_down, from_far, from_near, out, wide, terrain):
    gx = lax.axis_index("gx")
    gy = lax.axis_index("gy")
    odd = gy % 2 == 1
    lane8 = iota((8, LANES), 1)
    for rt in range(4):
        for group in range(3):
            at = (rt * 3 + group) * 8
            far, near = from_far[at : at + 8, :], from_near[at : at + 8, :]
            from_left, from_right = jnp.where(odd, near, far), jnp.where(odd, far, near)
            for s in range(min(16, PLANES - group * 16)):
                plane = group * 16 + s
                right_part = pltpu.roll(from_right, (LANES - 8 * s) % LANES, 1)
                left_part = pltpu.roll(from_left, (120 - 8 * s) % LANES, 1)
                halo = jnp.where(lane8 < 8, right_part, jnp.where(lane8 >= 120, left_part, 0.0))
                centre = strip(state, metric, from_up, from_down, plane, rt)
                if plane < 4 * L:
                    wide[plane, 0, rt * 8 : rt * 8 + 8, :] = centre
                    wide[plane, 1, rt * 8 : rt * 8 + 8, :] = halo
                else:
                    terrain[plane - 4 * L, 0, rt * 8 : rt * 8 + 8, :] = centre
                    terrain[plane - 4 * L, 1, rt * 8 : rt * 8 + 8, :] = halo

    row = iota((EXT, LANES), 0) + ROWS * gx - HALO
    lane = iota((EXT, LANES), 1)
    row_in = (row >= 0) & (row < N_X)
    last = lax.axis_size("gy") - 1
    halo_in = row_in & (((lane < 8) & (gy < last)) | ((lane >= 120) & (gy > 0)))
    for tile, inside in ((0, row_in), (1, halo_in)):
        inverse = 1.0 / jnp.where(inside, terrain[2, tile], 1.0)
        terrain[2, tile] = inverse
        terrain[3, tile] = jnp.where(inside, 0.5, 0.0)

    def substep(_, carry):
        for k in range(L):
            up, low = min(k + 1, L - 1), max(k - 1, 0)
            sigma = 1.0 - (k + 0.5) / L
            centre, halo = wide[24 + k, 0], wide[24 + k, 1]
            east = next_col(centre, halo, lane)
            west = prev_col(centre, halo, lane)
            for tile in range(2):
                here = (centre, halo)[tile]
                step = terrain[3, tile]
                press_z = (wide[24 + up, tile] - wide[24 + low, tile]) * (0.5 * terrain[2, tile])
                grad_x = (pltpu.roll(here, EXT - 1, 0) - pltpu.roll(here, 1, 0)) * 0.5
                grad_y = (east[tile] - west[tile]) * 0.5
                lean = sigma * press_z
                wide[k, tile] = wide[k, tile] - step * (grad_x - terrain[0, tile] * lean)
                wide[8 + k, tile] = wide[8 + k, tile] - step * (grad_y - terrain[1, tile] * lean)
                wide[16 + k, tile] = wide[16 + k, tile] - 0.5 * press_z
        for k in range(L):
            up, low = min(k + 1, L - 1), max(k - 1, 0)
            sigma = 1.0 - (k + 0.5) / L
            north = next_col(wide[8 + k, 0], wide[8 + k, 1], lane)
            south = prev_col(wide[8 + k, 0], wide[8 + k, 1], lane)
            for tile in range(2):
                wind = wide[k, tile]
                flat = pltpu.roll(wind, EXT - 1, 0) - pltpu.roll(wind, 1, 0) + north[tile] - south[tile]
                slope = terrain[0, tile] * (wide[up, tile] - wide[low, tile])
                slope = slope + terrain[1, tile] * (wide[8 + up, tile] - wide[8 + low, tile])
                rise = wide[16 + up, tile] - wide[16 + low, tile]
                spread = 0.5 * (flat + terrain[2, tile] * (rise - sigma * slope))
                wide[24 + k, tile] = wide[24 + k, tile] - terrain[3, tile] * spread
        return carry

    lax.fori_loop(0, SUB, substep, 0)
    for plane in range(4 * L):
        out[plane * ROWS : plane * ROWS + ROWS, :] = wide[plane, 0, HALO : HALO + ROWS, :]


def seated(seat):
    nest = 0
    for n in range(1, NESTS):
        nest = jnp.where(seat == SEAT[n], n, nest)
    return nest


def corner(placement, nest):
    both = placement[...]
    mine = iota(both.shape, 1) == nest
    one = [jnp.sum(jnp.where(mine & (iota(both.shape, 0) == d), both, 0.0)) for d in range(2)]
    return one[0].astype(jnp.int32), one[1].astype(jnp.int32)


def spread_kernel(got, placement, slots, store, sems):
    gx = lax.axis_index("gx")
    nest = seated(lax.axis_index("gy"))
    ox, oy = corner(placement, nest)
    lane = iota((THREE, LANES), 1)

    def line(col, b, c):
        return got[pl.ds((col // LANES) * SLOT + X_ROWS + 3 * c + b, 1), :]

    south = [[line(oy + b, b, c) for c in range(3)] for b in range(2)]
    north = [[line(oy + NORTH + b, b, c) for c in range(3)] for b in range(3)]
    even = jnp.concatenate(south[0] + north[0] + [north[2][0], north[2][2]], 0)
    odd = jnp.concatenate(south[1] + north[1] + [north[2][1], north[2][2]], 0)
    half = iota((8, LANES), 1) % ROWS < 8
    copies = [
        pltpu.make_async_copy(store.at[pl.ds(h * 4 * FINE, 4 * FINE)], slots.at[pl.ds(h * 4 * FINE, 4 * FINE)], sems.at[h])
        for h in range(2)
    ]
    for g in range(8):
        reach = 0
        for n in range(NESTS):
            reach = jnp.where(nest == n, (LANES * PIECE[n][g]) // R, reach)
        start = oy + reach
        low = start // LANES
        high = jnp.minimum(low + 1, 7)
        shift = start % LANES
        parts = []
        for a in range(2):
            near = got[pl.ds(pl.multiple_of(low * SLOT + a * THREE, 8), THREE), :]
            far = got[pl.ds(pl.multiple_of(high * SLOT + a * THREE, 8), THREE), :]
            parts.append(pltpu.roll(jnp.where(lane >= shift, near, far), (LANES + 64 * a - shift) % LANES, 1))
        store[g * FINE : g * FINE + THREE, :] = jnp.where(lane < 64, parts[0], parts[1])
        turn = ROWS * gx - ox - (ROWS * g) // R + 4 * LANES
        store[g * FINE + THREE : g * FINE + FINE, :] = jnp.where(
            half, pltpu.roll(even, turn % LANES, 1), pltpu.roll(odd, (turn + 8) % LANES, 1)
        )
        if g % 4 == 3:
            copies[g // 4].start()
    for h in range(2):
        copies[h].wait()


def merge_kernel(got, placement, west, east, along):
    nest = seated(lax.axis_index("gy"))
    ox, _ = corner(placement, nest)
    lane = iota((THREE, LANES), 1)

    def rows(row):
        return got[pl.ds(pl.multiple_of((row // ROWS) * FINE, 8), THREE), :]

    west[...] = jnp.where(lane < 64, rows(ox), rows(ox + 1))
    east[...] = jnp.where(lane < 64, rows(ox + EAST), rows(ox + EAST + 1))
    start = ox + (ROWS * lax.axis_index("gx")) // R
    low = start // ROWS
    high = jnp.minimum(low + 1, 7)
    near = got[pl.ds(pl.multiple_of(low * FINE + THREE, 8), 8), :]
    far = got[pl.ds(pl.multiple_of(high * FINE + THREE, 8), 8), :]
    along[...] = jnp.where(iota((8, LANES), 1) % 8 < ROWS * (low + 1) - start, near, far)


def third(value):
    return (value * 171) >> 9


def relax_kernel(moved, west, east, south, north, zones, out, store, sems):
    group = lax.axis_index("nest")
    gx = lax.axis_index("gx")
    gy = lax.axis_index("gy")
    nest = jnp.minimum(group, NESTS - 1)
    last_x = lax.axis_size("gx") - 1
    size = L * ROWS
    copies = [
        pltpu.make_async_copy((moved if f == 2 else store).at[pl.ds(f * size, size)], out.at[pl.ds(f * size, size)], sems.at[f])
        for f in range(4)
    ]

    @pl.when(group == NESTS)
    def _():
        plain = pltpu.make_async_copy(moved, out, sems.at[0])
        plain.start()
        plain.wait()

    @pl.when(group < NESTS)
    def _():
        copies[2].start()
        source = jnp.where(gx == 0, west[...], east[...])
        index = third(iota((THREE, LANES), 1) + (LANES * gy) % R)
        lines = [jnp.take_along_axis(source, index + 64 * a, axis=1) for a in range(2)]

        big_row, big_lane = iota((LANES, LANES), 0), iota((LANES, LANES), 1)
        need = third(big_row % ROWS + (ROWS * gx) % R)
        pick = ((big_row // ROWS == big_lane // ROWS) & (big_lane % 8 == need)).astype(F32)

        row, col = iota((ROWS, LANES), 0), iota((ROWS, LANES), 1)
        row_pos, col_pos = (row + ROWS * gx).astype(F32), (col + LANES * gy).astype(F32)
        own = jnp.where(iota((4, NESTS), 1) == nest, zones[...].astype(F32), 0.0)
        widths = jnp.sum(own, axis=1, keepdims=True)
        weight = jnp.zeros((ROWS, LANES), F32)
        for edge, dist in enumerate((row_pos, N_X - 1 - row_pos, col_pos, N_Y - 1 - col_pos)):
            width = jnp.broadcast_to(widths[edge : edge + 1, :], (ROWS, LANES))
            weight = jnp.maximum(weight, jnp.maximum((width - dist) / width, 0.0))
        weight = jnp.where(group < NESTS, weight, 0.0)
        in_x = ((gx == 0) & (row < W_MAX)) | ((gx == last_x) & (row >= ROWS - W_MAX))
        split = jnp.where(gx == 0, 3, ROWS - 2)

        lane8, row8 = iota((8, LANES), 1), iota((8, LANES), 0)
        first_half = lane8 % ROWS < 8
        for c, field in enumerate((0, 1, 3)):
            pair = jnp.broadcast_to(south[c : c + 1, :], (8, LANES))
            low = jnp.where(first_half == (row8 < 3), pair, 0.0)
            low = jnp.where(row8 < W_MAX, low, 0.0)
            pair = jnp.broadcast_to(north[3 + c : 4 + c, :], (8, LANES))
            last = jnp.broadcast_to(north[(6, 6, 7)[c] : (7, 7, 8)[c], :], (8, LANES))
            last = jnp.where(first_half == (c != 1), last, 0.0)
            high = jnp.where(first_half == (row8 < 4), pair, 0.0)
            high = jnp.where(row8 == 7, last, jnp.where(row8 >= 3, high, 0.0))
            table = jnp.concatenate([low, jnp.zeros((112, LANES), F32), high], 0)
            along = lax.dot_general(pick, table, (((1,), (1,)), ((), ())), precision=HIGH, preferred_element_type=F32)
            for k in range(L):
                plane = c * L + k
                line0 = jnp.broadcast_to(lines[0][plane : plane + 1, :], (ROWS, LANES))
                line1 = jnp.broadcast_to(lines[1][plane : plane + 1, :], (ROWS, LANES))
                target = jnp.where(in_x, jnp.where(row < split, line0, line1), along[k * ROWS : k * ROWS + ROWS, :])
                at = (field * L + k) * ROWS
                value = moved[at : at + ROWS, :]
                store[at : at + ROWS, :] = value + weight * (target - value)
            copies[field].start()
        for f in range(4):
            copies[f].wait()


ANY_SPEC = pl.BlockSpec(memory_space=pl.ANY)


def call(kernel, specs, outs, scratch=(), near=True):
    places = near if isinstance(near, tuple) else (near,) * len(outs)
    many = tuple(pltpu.VMEM(shape, F32) if near_by else jax.ShapeDtypeStruct(shape, F32) for shape, near_by in zip(outs, places))
    run = pl.pallas_call(
        kernel,
        in_specs=list(specs),
        out_specs=tuple(VMEM_SPEC if near_by else ANY_SPEC for near_by in places),
        out_shape=many,
        scratch_shapes=list(scratch),
    )

    def placed(*args):
        return run(*(a if s is ANY_SPEC else pltpu.with_memory_space_constraint(a, s.memory_space) for a, s in zip(args, specs)))

    return placed


def local(state, metric, placement, zones):
    return whole(state, metric, placement.T, zones.T)


def whole(state, metric, placement, zones):
    flat = state.reshape(4 * L * ROWS, LANES)
    ground = metric.reshape(3 * ROWS, LANES)
    V, A = VMEM_SPEC, ANY_SPEC
    axes = ("nest", "gx", "gy")
    DMA = pltpu.SemaphoreType.DMA

    def pairs_of(axis, step, groups):
        pairs = []
        for n in groups:
            for x in range(8):
                for y in range(8):
                    to = (x + step, y) if axis == 0 else (x, y + step)
                    if 0 <= to[axis] < 8:
                        pairs.append(((n * 8 + x) * 8 + y, (n * 8 + to[0]) * 8 + to[1]))
        return pairs

    def shifted(value, axis, step, groups):
        return lax.ppermute(value, axes, pairs_of(axis, step, groups))

    def rows_halo(flat, ground, groups):
        to_up, to_down = call(edge_kernel, (V, V), [(PLANES * 8, LANES)] * 2)(flat, ground)
        return shifted(to_down, 0, 1, groups), shifted(to_up, 0, -1, groups)

    kept = [(96, LANES)] * 2 + [(PLANES * 8, LANES)] * 2 + [(4 * L * ROWS, LANES), (3 * ROWS, LANES)]

    def packed(flat, ground, from_up, from_down):
        return call(pack_kernel, (V,) * 4, kept)(flat, ground, from_up, from_down)

    def as_parent(flat, ground, placement):
        mine = (NESTS,)
        slots, info = call(
            select_kernel,
            (A, A),
            [(8, SLOT, LANES), (8, LANES)],
            [
                pltpu.VMEM((3 * L * ROWS, LANES), F32),
                pltpu.VMEM((8, SLOT, LANES), F32),
                pltpu.SMEM((2, NESTS), jnp.int32),
                DMA((4,)),
                DMA((2,)),
            ],
            near=(False, True),
        )(flat, pltpu.with_memory_space_constraint(placement, pltpu.HBM))
        first = lax.all_to_all(slots, "gy", 0, 0).reshape(8 * SLOT, LANES)
        from_up, from_down = rows_halo(flat, ground, mine)
        (second,) = call(
            spread_kernel,
            (V, V),
            [(8 * FINE, LANES)],
            [pltpu.VMEM((8 * FINE, LANES), F32), DMA((2,))],
            near=False,
        )(first, info)
        arrived = lax.all_to_all(second.reshape(8, FINE, LANES), "gx", 0, 0).reshape(8 * FINE, LANES)
        halos = packed(flat, ground, from_up, from_down)
        parts = call(merge_kernel, (V, V), [(THREE, LANES), (THREE, LANES), (8, LANES)])(arrived, info)
        return (*halos, *parts)

    def as_nest(flat, ground, placement):
        others = range(NESTS)
        from_up, from_down = rows_halo(flat, ground, others)
        halos = packed(flat, ground, from_up, from_down)
        none = jnp.zeros((THREE, LANES), F32)
        return (*halos, none, none, none[:8])

    far, near, from_up, from_down, flat, ground, across, beyond, along = lax.cond(
        lax.axis_index("nest") == NESTS, as_parent, as_nest, flat, ground, placement
    )

    def send(value, place):
        pairs = []
        for n in range(NESTS):
            for g in range(8):
                x, y = place(g, PIECE[n][g])
                pairs.append(((NESTS * 8 + g) * 8 + SEAT[n], (n * 8 + x) * 8 + y))
        return lax.ppermute(value, axes, pairs)

    west = send(across, lambda g, q: (0, q))
    east = send(beyond, lambda g, q: (7, q))
    top = send(along, lambda g, q: (g, 7))
    bottom = send(along, lambda g, q: (g, 0))

    def swapped(value, first):
        pairs = []
        for n in range(NESTS + 1):
            for x in range(8):
                for y in range(first, 7, 2):
                    a = (n * 8 + x) * 8 + y
                    pairs += [(a, a + 1), (a + 1, a)]
        return lax.ppermute(value, axes, pairs)

    from_far = swapped(far, 1)
    from_near = swapped(near, 0)
    (moved,) = call(
        advance_kernel,
        (V,) * 6,
        [(4 * L * ROWS, LANES)],
        [pltpu.VMEM((4 * L, 2, EXT, LANES), F32), pltpu.VMEM((4, 2, EXT, LANES), F32)],
    )(flat, ground, from_up, from_down, from_far, from_near)
    (result,) = call(
        relax_kernel,
        (V,) * 6,
        [(4 * L * ROWS, LANES)],
        [pltpu.VMEM((4 * L * ROWS, LANES), F32), DMA((4,))],
        near=False,
    )(moved, west, east, bottom, top, zones)
    return result.reshape(state.shape)


def solution(mesh):
    return jax.shard_map(
        local,
        mesh=mesh,
        in_specs=(P("nest", None, None, "gx", "gy"), P("nest", None, "gx", "gy"), P(), P()),
        out_specs=P("nest", None, None, "gx", "gy"),
        check_vma=False,
    )
```
